256 devices in a mesh: row: 16 (over z_lo, y, core), col: 16 (over x, z_hi).
Axes of the slice: x: 4, y: 4, z: 8 (z_hi: 4, z_lo: 2; z = z_hi * 2 + z_lo), core: 2. Of those that a mesh axis runs over, the one named last changes fastest.
Arguments:
- positions: float32 [3, 262144], P(None, ('col', 'row')), may hold values from 0 to 16
- velocity: float32 [3, 262144], P(None, ('col', 'row')), may hold values from -6 to 6
- applied: float32 [3, 262144], P(None, ('col', 'row')), may hold values from -12 to 12
- suscept: float32 [262144], P(('col', 'row')), may hold values from 0.05 to 0.3
- contact_owner: int32 [16, 16, 16, 512], P('col', 'row'), may hold values from 0 to 1023
- contact_partner: int32 [16, 16, 16, 512], P('col', 'row'), may hold values from 0 to 1023
- contact_count: int32 [16, 16, 16], P('col', 'row'), may hold values from 1 to 512, as said below
Outputs:
- moments: float32 [3, 262144], P(None, ('col', 'row'))
- forces: float32 [3, 262144], P(None, ('col', 'row'))
The draws below stay inside these ranges and needn't reach their ends.
Inputs may be any that keep to these rules, and one draw needn't show every extreme that they name: `contact_count`: in every draw one column receives full blocks of 512 live slots from every device; the other columns' blocks are filled to different depths.
All inputs are finite; a program needn't handle non-finite values.
Results may differ from the reference program's by a relative error of at most 0.0003.
Values sent between devices are 32-bit elements; how exact they have to be, the bound alone decides.
A program may use at most 64 MiB of HBM per device.

```python
import math
import jax
import jax.numpy as jnp
from jax import lax

PART_DEV = 1024
ITERS = 2
CAP = 512
NPART = 262144
N_ROW = 16
N_COL = 16


def draw_contact_count(key, part):
    key_heavy, key_upper, key_counts = jax.random.split(jax.random.fold_in(key, 17), 3)
    heavy_col = jax.random.randint(key_heavy, (), 0, N_COL)
    upper_bound = jax.random.randint(key_upper, (N_COL,), CAP // 2, CAP + 1)
    drawn_counts = jax.random.randint(key_counts, (N_COL, N_ROW, N_COL), 1, upper_bound[None, None, :] + 1)
    col_ids = jnp.arange(N_COL)
    return jnp.where((col_ids == heavy_col)[None, None, :], CAP, drawn_counts).astype(jnp.int32)


def plant(drawn, own_key, low, top_value):
    extent = drawn.shape
    index_at = [jax.random.randint(jax.random.fold_in(own_key, axis), (), 0, extent[axis]) for axis in range(len(extent))]
    drawn = drawn.at[tuple(index_at)].set(low)
    longest = extent.index(max(extent))
    index_at[longest] = (index_at[longest] + 1) % extent[longest]
    return drawn.at[tuple(index_at)].set(top_value)


def levels(stream_key, extent, cuts, smallest, largest):
    gain = 1.0
    for axis_at, parts in cuts:
        steps = jax.random.uniform(jax.random.fold_in(jax.random.fold_in(stream_key, 6), axis_at), (parts,), jnp.float32, smallest / len(cuts), largest / len(cuts))
        gain = gain * jnp.repeat(jnp.exp(steps), extent[axis_at] // parts).reshape((-1,) + (1,) * (len(extent) - 1 - axis_at))
    return gain


def normal_values(own_key, extent, scale, bound, pieces=(), held_as=jnp.bfloat16):
    drawn = scale * jax.random.normal(own_key, extent, jnp.float32)
    if pieces:
        drawn = drawn * levels(own_key, extent, pieces, -0.22, 0.18)
    return jnp.clip(drawn, -bound, bound).astype(held_as)


def setup_inputs(seed: int = 0) -> dict:
    keys = jax.random.split(jax.random.key(seed), 8)
    return {
        "positions": jnp.clip(16.0 * jax.random.uniform(keys[0], (3, NPART), jnp.float32) ** levels(keys[0], (3, NPART), ((1, 256),), -0.2, 0.2), 0.0, 16.0),
        "velocity": normal_values(keys[1], (3, NPART), 1.0, 6.0, ((1, 256),), jnp.float32),
        "applied": normal_values(keys[2], (3, NPART), 2.0, 12.0, ((1, 256),), jnp.float32),
        "suscept": jnp.clip(jnp.exp(math.log(0.3) - 1.7917595 * jax.random.uniform(keys[3], (NPART,), jnp.float32) ** levels(keys[3], (NPART,), ((0, 256),), -0.2, 0.2)), 0.05, 0.3),
        "contact_owner": plant(jax.random.randint(keys[4], (N_COL, N_ROW, N_COL, CAP), 0, PART_DEV), jax.random.fold_in(keys[4], 1), 0, PART_DEV - 1).astype(jnp.int32),
        "contact_partner": plant(jax.random.randint(keys[5], (N_COL, N_ROW, N_COL, CAP), 0, PART_DEV), jax.random.fold_in(keys[5], 1), 0, PART_DEV - 1).astype(jnp.int32),
        "contact_count": draw_contact_count(jax.random.fold_in(keys[7], 71), 0),
    }


def dipole_block(target_pos, target_ids, source_pos, source_mom, source_ids):
    offset = target_pos[:, :, None] - source_pos[:, None, :]
    radius_sq = lax.optimization_barrier(jnp.sum(offset * offset, axis=0)) + 1.0
    inverse_r = lax.rsqrt(radius_sq)
    inverse_cube = inverse_r * inverse_r * inverse_r
    inverse_fifth = inverse_cube * inverse_r * inverse_r
    keep_mask = target_ids[:, None] != source_ids[None, :]
    projection = lax.optimization_barrier(jnp.sum(offset * source_mom[:, None, :], axis=0))
    radial_coef = jnp.where(keep_mask, 3.0 * projection * inverse_fifth, 0.0)
    direct_coef = jnp.where(keep_mask, inverse_cube, 0.0)
    return lax.optimization_barrier(jnp.sum(radial_coef[None] * offset, axis=2)) - lax.optimization_barrier(jnp.sum(direct_coef[None] * source_mom[:, None, :], axis=2))

def column_field(column_pos, column_mom):
    column_len = column_pos.shape[1]
    block_len = math.gcd(column_len, 512)
    nblocks = column_len // block_len
    all_ids = jnp.arange(column_len, dtype=jnp.int32)
    target_blocks = (column_pos.reshape(3, nblocks, block_len).transpose(1, 0, 2), all_ids.reshape(nblocks, block_len))

    def per_block(target_block):
        return dipole_block(target_block[0], target_block[1], column_pos, column_mom, all_ids)
    result_blocks = lax.map(per_block, target_blocks)
    return result_blocks.transpose(1, 0, 2).reshape(3, column_len)

def pair_force(one_side, other_side):
    separation = one_side[0:3] - other_side[0:3]
    distance = jnp.sqrt(lax.optimization_barrier(jnp.sum(separation * separation, axis=0)) + 1.0)
    normal = separation / distance
    mom_one = one_side[6:9]
    mom_other = other_side[6:9]
    along_one = lax.optimization_barrier(jnp.sum(mom_one * normal, axis=0))
    along_other = lax.optimization_barrier(jnp.sum(mom_other * normal, axis=0))
    mom_dot = lax.optimization_barrier(jnp.sum(mom_one * mom_other, axis=0))
    magnetic = 3.0 * (along_one * mom_other + along_other * mom_one + (mom_dot - 5.0 * along_one * along_other) * normal)
    spring = -0.03 * (distance - 1.0) * normal
    rel_speed = lax.optimization_barrier(jnp.sum((one_side[3:6] - other_side[3:6]) * normal, axis=0))
    damping = -0.5 * rel_speed * normal
    return magnetic + spring + damping

def reference(positions, velocity, applied, suscept, contact_owner, contact_partner, contact_count):
    column_len = PART_DEV * N_ROW
    pos_cols = positions.reshape(3, N_COL, column_len).transpose(1, 0, 2)
    moments = suscept[None, :] * applied
    for iteration in range(ITERS):
        mom_cols = moments.reshape(3, N_COL, column_len).transpose(1, 0, 2)
        field_cols = lax.map(lambda pair_cols: column_field(pair_cols[0], pair_cols[1]), (pos_cols, mom_cols))
        field_sum = field_cols.transpose(1, 0, 2).reshape(3, N_COL * column_len)
        moments = suscept[None, :] * (applied + field_sum)
    col_ids = jnp.arange(N_COL, dtype=jnp.int32)
    row_ids = jnp.arange(N_ROW, dtype=jnp.int32)
    owner_global = (col_ids[:, None, None, None] * N_ROW + row_ids[None, :, None, None]) * PART_DEV + contact_owner
    partner_global = (col_ids[None, None, :, None] * N_ROW + row_ids[None, :, None, None]) * PART_DEV + contact_partner
    slot_ids = jnp.arange(CAP, dtype=jnp.int32)
    live_mask = (slot_ids[None, None, None, :] < contact_count[:, :, :, None]).astype(jnp.float32).reshape(-1)
    state_rows = jnp.concatenate([positions, velocity, moments], axis=0)
    owner_flat = owner_global.reshape(-1).astype(jnp.int32)
    partner_flat = partner_global.reshape(-1).astype(jnp.int32)
    owner_rows = jnp.take(state_rows, owner_flat, axis=1)
    partner_rows = jnp.take(state_rows, partner_flat, axis=1)
    slot_force = pair_force(owner_rows, partner_rows) * live_mask[None, :]
    forces = jnp.zeros_like(positions).at[:, owner_flat].add(slot_force).at[:, partner_flat].add(-slot_force)
    return (moments, forces)
```

```python
import functools

import jax
import jax.numpy as jnp
from jax import lax
from jax.experimental import pallas as pl
from jax.experimental.pallas import tpu as pltpu
from jax.sharding import PartitionSpec as P

F32 = jnp.float32
BF16 = jnp.bfloat16
MESH = pl.DeviceIdType.MESH
CENTRE = 8.0
SRC_BLOCK = 512
TGT_BLOCK = 256


def vmem_specs(count):
    return [pl.BlockSpec(memory_space=pltpu.VMEM)] * count


def peers(axis):
    size = lax.axis_size(axis)
    me = lax.axis_index(axis)
    return [
        (step, lax.rem(me + step, size), lax.rem(me + size - step, size))
        for step in range(1, size)
    ], me


def enter(axes):
    barrier = pltpu.get_barrier_semaphore()
    total = 0
    for axis in axes:
        others, unused = peers(axis)
        for step, target, source in others:
            pl.semaphore_signal(barrier, inc=1, device_id={axis: target}, device_id_type=MESH)
        total += len(others)
    pl.semaphore_wait(barrier, total)


def exchange(axis, source_of, out_ref, send_sem, recv_sem):
    others, me = peers(axis)
    copies = []
    for step, target, source in others:
        copy = pltpu.make_async_remote_copy(
            src_ref=source_of(target),
            dst_ref=out_ref.at[me],
            send_sem=send_sem.at[step],
            recv_sem=recv_sem.at[step],
            device_id={axis: target},
            device_id_type=MESH,
        )
        copy.start()
        copies.append(copy)
    own = pltpu.make_async_copy(source_of(me), out_ref.at[me], send_sem.at[0])
    own.start()
    return copies + [own]


def first_exchange(row_ref, col_ref, list_ref, row_out, col_out, list_out, send_sem, recv_sem):
    enter(("row", "col"))
    copies = exchange("row", lambda t: row_ref, row_out, send_sem.at[0], recv_sem.at[0])
    copies += exchange("col", lambda t: list_ref.at[t], list_out, send_sem.at[1], recv_sem.at[1])
    copies += exchange("col", lambda t: col_ref, col_out, send_sem.at[2], recv_sem.at[2])
    for copy in copies:
        copy.wait()


def one_exchange(axis, block_ref, out_ref, send_sem, recv_sem):
    enter((axis,))
    for copy in exchange(axis, lambda t: block_ref, out_ref, send_sem, recv_sem):
        copy.wait()


def gather_blocks(block, axis, collective_id, size):
    return pl.pallas_call(
        functools.partial(one_exchange, axis),
        out_shape=jax.ShapeDtypeStruct((size,) + block.shape, block.dtype),
        in_specs=vmem_specs(1),
        out_specs=pl.BlockSpec(memory_space=pltpu.VMEM),
        scratch_shapes=[pltpu.SemaphoreType.DMA((size,)), pltpu.SemaphoreType.DMA((size,))],
        compiler_params=pltpu.CompilerParams(collective_id=collective_id, has_side_effects=True),
        name="gather_" + axis + str(collective_id),
    )(block)


def pieces(value, count):
    out = []
    for unused in range(count):
        head = value.astype(BF16)
        wide = head.astype(F32)
        out.append(wide)
        value = value - wide
    return out


def target_rows(pos):
    first, second, third = pieces(-2.0 * pos, 3)
    norm = jnp.sum(pos * pos, axis=0, keepdims=True) + 1.0
    one = jnp.ones_like(norm)
    rows = [first, second, third, first, second, first, one, one, one] + pieces(norm, 3)
    return jnp.concatenate(rows, axis=0).astype(BF16)


def source_rows(pos):
    first, second, third = pieces(pos, 3)
    norm = jnp.sum(pos * pos, axis=0, keepdims=True)
    one = jnp.ones_like(norm)
    rows = [first, first, first, second, second, third] + pieces(norm, 3) + [one, one, one]
    return jnp.concatenate(rows, axis=0).astype(BF16)


def source_weights(pos, mom):
    norm = jnp.sum(pos * pos, axis=0, keepdims=True)
    along = jnp.sum(pos * mom, axis=0, keepdims=True)
    terms = jnp.concatenate(
        [mom, pos[0:1] * mom, pos[1:2] * mom, pos[2:3] * mom, norm * mom, along * pos], axis=0
    )
    return jnp.concatenate(pieces(terms, 3), axis=0).astype(BF16)


def combine(acc, pos):
    sums = acc[0:18] + (acc[18:36] + acc[36:54])
    x, y, z = pos[0:1], pos[1:2], pos[2:3]
    mom = sums[0:3]
    by_x, by_y, by_z = sums[3:6], sums[6:9], sums[9:12]
    norm_mom, along_pos = sums[12:15], sums[15:18]
    inner = x * mom[0:1] + y * mom[1:2] + z * mom[2:3]
    trace = by_x[0:1] + by_y[1:2] + by_z[2:3]
    crossed = jnp.concatenate(
        [x * by[0:1] + y * by[1:2] + z * by[2:3] for by in (by_x, by_y, by_z)], axis=0
    )
    radial = pos * (inner - trace) - crossed + along_pos
    norm = jnp.sum(pos * pos, axis=0, keepdims=True) + 1.0
    direct = norm * mom + norm_mom - 2.0 * (x * by_x + y * by_y + z * by_z)
    return 3.0 * radial - direct


def field_kernel(passes, own_ref, pos_ref, mom_ref, field_ref, rows_ref, weights_ref, target_ref, acc_ref):
    parts, unused, part_len = pos_ref.shape
    mom_at = 3 if pos_ref.shape == mom_ref.shape else 0

    @pl.loop(0, parts)
    def _(part):
        at = pl.ds(pl.multiple_of(part * part_len, part_len), part_len)
        pos = pos_ref[part, 0:3, :]
        mom = mom_ref[part, mom_at : mom_at + 3, :]
        rows_ref[:, at] = source_rows(pos)
        weights_ref[:, at] = source_weights(pos, mom)

    own_pos = own_ref[0:3, :]
    target_ref[...] = target_rows(own_pos)
    acc_ref[...] = jnp.zeros_like(acc_ref)

    @pl.loop(0, parts * part_len // SRC_BLOCK)
    def _(block):
        at = pl.ds(pl.multiple_of(block * SRC_BLOCK, SRC_BLOCK), SRC_BLOCK)
        rows = rows_ref[:, at]
        weights = weights_ref[:, at]
        for start in range(0, part_len, TGT_BLOCK):
            to = slice(start, start + TGT_BLOCK)
            radius_sq = lax.dot_general(
                rows, target_ref[:, to], (((0,), (0,)), ((), ())), preferred_element_type=F32
            )
            inverse = lax.rsqrt(radius_sq)
            square = inverse * inverse
            fifth = square * square * inverse
            head = fifth.astype(BF16)
            added = jnp.dot(weights, head, preferred_element_type=F32)
            if passes == 2:
                tail = (fifth - head.astype(F32)).astype(BF16)
                added = added + jnp.dot(weights, tail, preferred_element_type=F32)
            acc_ref[:, to] += added

    field_ref[0:3, :] = combine(acc_ref[...], own_pos)


def field_of(passes, own, pos_all, mom_all):
    parts, unused, part_len = pos_all.shape
    total = parts * part_len
    return pl.pallas_call(
        functools.partial(field_kernel, passes),
        out_shape=jax.ShapeDtypeStruct((3, part_len), F32),
        in_specs=vmem_specs(3),
        out_specs=pl.BlockSpec(memory_space=pltpu.VMEM),
        scratch_shapes=[
            pltpu.VMEM((24, total), BF16),
            pltpu.VMEM((54, total), BF16),
            pltpu.VMEM((24, part_len), BF16),
            pltpu.VMEM((54, part_len), F32),
        ],
        name="field" + str(passes),
    )(own, pos_all, mom_all)


def picked(table, high, low):
    out = None
    for group, row in enumerate(table):
        found = jnp.take_along_axis(row, low, axis=1)
        out = found if out is None else jnp.where(high == group, found, out)
    return out


def pair_force(mine, other):
    sep = [mine[k] - other[k] for k in range(3)]
    vel = [mine[3 + k] - other[3 + k] for k in range(3)]
    m_one = mine[6:9]
    m_two = other[6:9]

    def dot(a, b):
        return a[0] * b[0] + a[1] * b[1] + a[2] * b[2]

    radius_sq = dot(sep, sep) + 1.0
    inverse = lax.rsqrt(radius_sq)
    distance = radius_sq * inverse
    normal = [s * inverse for s in sep]
    one = dot(m_one, normal)
    two = dot(m_two, normal)
    radial = 3.0 * (dot(m_one, m_two) - 5.0 * one * two)
    radial = radial - 0.03 * (distance - 1.0) - 0.5 * dot(vel, normal)
    return [3.0 * (one * m_two[k] + two * m_one[k]) + radial * normal[k] for k in range(3)]


def contact_kernel(own_ref, mom_ref, col_ref, mom_all_ref, list_ref, back_ref, out_ref, acc_ref):
    columns = col_ref.shape[0]
    half = list_ref.shape[1] // 2
    acc_ref[...] = jnp.zeros_like(acc_ref)

    def table(read):
        return [jnp.broadcast_to(read(slice(g * 128, g * 128 + 128)), (8, 128)) for g in range(8)]

    @pl.loop(0, columns)
    def _(column):
        here = list_ref[column]
        back = back_ref[column]
        my_ids = jnp.concatenate([here[:half], back[half:]], axis=0)
        other_ids = jnp.concatenate([here[half:], back[:half]], axis=0)
        live = my_ids >= 0
        live = jnp.logical_and(live, other_ids >= 0)
        my_high, my_low = my_ids >> 7, my_ids & 127
        other_high, other_low = other_ids >> 7, other_ids & 127
        mine, other = [], []
        for k in range(9):
            if k < 6:
                mine.append(picked(table(lambda s: own_ref[k : k + 1, s]), my_high, my_low))
                other.append(
                    picked(table(lambda s: col_ref[column, k : k + 1, s]), other_high, other_low)
                )
            else:
                j = k - 6
                mine.append(picked(table(lambda s: mom_ref[j : j + 1, s]), my_high, my_low))
                other.append(
                    picked(table(lambda s: mom_all_ref[column, j : j + 1, s]), other_high, other_low)
                )
        force = [jnp.where(live, f, 0.0) for f in pair_force(mine, other)]
        split = [p for f in force for p in pieces(f, 3)]
        group_ids = lax.broadcasted_iota(jnp.int32, (8, 128), 0)
        lane_ids = lax.broadcasted_iota(jnp.int32, (128, 128), 0)
        left, right = [], []
        for k in range(8):
            hit = jnp.broadcast_to(my_high[k : k + 1], (8, 128)) == group_ids
            left.append(
                jnp.concatenate(
                    [jnp.where(hit, jnp.broadcast_to(p[k : k + 1], (8, 128)), 0.0) for p in split], axis=0
                ).astype(BF16)
            )
            same = jnp.broadcast_to(my_low[k : k + 1], (128, 128)) == lane_ids
            right.append(jnp.where(same, 1.0, 0.0).astype(BF16))
        acc_ref[...] += lax.dot_general(
            jnp.concatenate(left, axis=1),
            jnp.concatenate(right, axis=1),
            (((1,), (1,)), ((), ())),
            preferred_element_type=F32,
        )

    for k in range(3):
        base = 24 * k
        total = acc_ref[base : base + 8] + (acc_ref[base + 8 : base + 16] + acc_ref[base + 16 : base + 24])
        for g in range(8):
            out_ref[k : k + 1, g * 128 : g * 128 + 128] = total[g : g + 1]


def contact_forces(own, mom, col_all, mom_all, lists, back):
    return pl.pallas_call(
        contact_kernel,
        out_shape=jax.ShapeDtypeStruct((3, own.shape[1]), F32),
        in_specs=vmem_specs(6),
        out_specs=pl.BlockSpec(memory_space=pltpu.VMEM),
        scratch_shapes=[pltpu.VMEM((72, 128), F32)],
        name="contacts",
    )(own, mom, col_all, mom_all, lists, back)


def on_device(positions, velocity, applied, suscept, contact_owner, contact_partner, contact_count):
    rows = lax.axis_size("row")
    cols = lax.axis_size("col")
    length = positions.shape[1]
    slots = contact_owner.shape[3]
    start = suscept[None, :] * applied
    centred = positions - CENTRE
    row_block = jnp.concatenate([centred, start], axis=0)
    col_block = jnp.concatenate([centred, velocity], axis=0)
    live = jnp.arange(slots, dtype=jnp.int32)[None, :] < contact_count.reshape(cols, 1)
    owners = jnp.where(live, contact_owner.reshape(cols, slots), -1).reshape(cols, slots // 128, 128)
    partners = jnp.where(live, contact_partner.reshape(cols, slots), -1).reshape(cols, slots // 128, 128)
    lists = jnp.concatenate([owners, partners], axis=1)

    row_all, col_all, back = pl.pallas_call(
        first_exchange,
        out_shape=(
            jax.ShapeDtypeStruct((rows, 6, length), F32),
            jax.ShapeDtypeStruct((cols, 6, length), F32),
            jax.ShapeDtypeStruct(lists.shape, jnp.int32),
        ),
        in_specs=vmem_specs(3),
        out_specs=tuple(vmem_specs(3)),
        scratch_shapes=[
            pltpu.SemaphoreType.DMA((3, max(rows, cols))),
            pltpu.SemaphoreType.DMA((3, max(rows, cols))),
        ],
        compiler_params=pltpu.CompilerParams(collective_id=0, has_side_effects=True),
        name="first_exchange",
    )(row_block, col_block, lists)

    field = field_of(2, row_block, row_all, row_all)
    moments = suscept[None, :] * (applied + (field + start))
    mom_row = gather_blocks(moments, "row", 1, rows)
    field = field_of(2, row_block, row_all, mom_row)
    moments = suscept[None, :] * (applied + (field + moments))
    mom_col = gather_blocks(moments, "col", 2, cols)
    forces = contact_forces(col_block, moments, col_all, mom_col, lists, back)
    return (moments, forces)


def solution(mesh):
    placed = (
        P(None, ("col", "row")),
        P(None, ("col", "row")),
        P(None, ("col", "row")),
        P(("col", "row")),
        P("col", "row", None, None),
        P("col", "row", None, None),
        P("col", "row", None),
    )
    return jax.shard_map(
        on_device,
        mesh=mesh,
        in_specs=placed,
        out_specs=(P(None, ("col", "row")), P(None, ("col", "row"))),
        check_vma=False,
    )
```

```python
import functools

import jax
import jax.numpy as jnp
from jax import lax
from jax.experimental import pallas as pl
from jax.experimental.pallas import tpu as pltpu
from jax.sharding import PartitionSpec as P

F32 = jnp.float32
BF16 = jnp.bfloat16
MESH = pl.DeviceIdType.MESH
CENTRE = 8.0
SRC_BLOCK = 512
ROW_SHAPE = (2, 4, 2)
TGT_BLOCK = 256


def vmem_specs(count):
    return [pl.BlockSpec(memory_space=pltpu.VMEM)] * count


def row_steps(step):
    depth, height, cores = ROW_SHAPE
    me = lax.axis_index("row")
    core, rest = lax.rem(me, cores), lax.div(me, cores)
    y, z = lax.rem(rest, height), lax.div(rest, height)
    core_by, rest_by = lax.rem(step, cores), lax.div(step, cores)
    turn, z_by = lax.rem(rest_by, height), lax.div(rest_by, height)
    y_by = turn + lax.div(turn, 2) - 2 * lax.div(turn, 3)

    def at(sign):
        new_z = lax.rem(z + depth + sign * z_by, depth)
        new_y = lax.rem(y + height + sign * y_by, height)
        new_core = lax.rem(core + cores + sign * core_by, cores)
        return (new_z * height + new_y) * cores + new_core

    return at(1), at(-1)


def col_steps(step):
    size = lax.axis_size("col")
    me = lax.axis_index("col")
    return lax.rem(me + step, size), lax.rem(me + size - step, size)


def each_step(axis, body):
    lax.fori_loop(1, lax.axis_size(axis), lambda step, carry: (body(step), carry)[1], 0)


def enter():
    barrier = pltpu.get_barrier_semaphore()

    def signal_row(step):
        pl.semaphore_signal(barrier, inc=1, device_id={"row": row_steps(step)[0]}, device_id_type=MESH)

    def signal_col(step):
        pl.semaphore_signal(barrier, inc=1, device_id={"col": col_steps(step)[0]}, device_id_type=MESH)

    each_step("row", signal_row)
    each_step("col", signal_col)
    pl.semaphore_wait(barrier, lax.axis_size("row") + lax.axis_size("col") - 2)


def pieces(value, count):
    out = []
    for unused in range(count):
        head = value.astype(BF16)
        wide = head.astype(F32)
        out.append(wide)
        value = value - wide
    return out


def target_rows(pos):
    first, second, third = pieces(-2.0 * pos, 3)
    norm = jnp.sum(pos * pos, axis=0, keepdims=True) + 1.0
    one = jnp.ones_like(norm)
    rows = [first, second, third, first, second, first, one, one, one] + pieces(norm, 3)
    return jnp.concatenate(rows, axis=0).astype(BF16)


def source_rows(pos):
    first, second, third = pieces(pos, 3)
    norm = jnp.sum(pos * pos, axis=0, keepdims=True)
    one = jnp.ones_like(norm)
    rows = [first, first, first, second, second, third] + pieces(norm, 3) + [one, one, one]
    return jnp.concatenate(rows, axis=0).astype(BF16)


def source_weights(pos, mom):
    norm = jnp.sum(pos * pos, axis=0, keepdims=True)
    along = jnp.sum(pos * mom, axis=0, keepdims=True)
    terms = jnp.concatenate(
        [mom, pos[0:1] * mom, pos[1:2] * mom, pos[2:3] * mom, norm * mom, along * pos], axis=0
    )
    return jnp.concatenate(pieces(terms, 3), axis=0).astype(BF16)


def combine(acc, pos):
    sums = acc[0:18] + (acc[18:36] + acc[36:54])
    x, y, z = pos[0:1], pos[1:2], pos[2:3]
    mom = sums[0:3]
    by_x, by_y, by_z = sums[3:6], sums[6:9], sums[9:12]
    norm_mom, along_pos = sums[12:15], sums[15:18]
    inner = x * mom[0:1] + y * mom[1:2] + z * mom[2:3]
    trace = by_x[0:1] + by_y[1:2] + by_z[2:3]
    crossed = jnp.concatenate(
        [x * by[0:1] + y * by[1:2] + z * by[2:3] for by in (by_x, by_y, by_z)], axis=0
    )
    radial = pos * (inner - trace) - crossed + along_pos
    norm = jnp.sum(pos * pos, axis=0, keepdims=True) + 1.0
    direct = norm * mom + norm_mom - 2.0 * (x * by_x + y * by_y + z * by_z)
    return 3.0 * radial - direct


def add_field(rows_ref, weights_ref, target_ref, acc_ref, first, count, targets):
    sums = {}
    for start in range(0, count, SRC_BLOCK):
        at = pl.ds(pl.multiple_of(first + start, SRC_BLOCK), SRC_BLOCK)
        rows = rows_ref[:, at]
        weights = weights_ref[:, at]
        for low in range(targets[0], targets[1], TGT_BLOCK):
            to = slice(low, low + TGT_BLOCK)
            radius_sq = lax.dot_general(
                rows, target_ref[:, to], (((0,), (0,)), ((), ())), preferred_element_type=F32
            )
            inverse = lax.rsqrt(radius_sq)
            square = inverse * inverse
            fifth = square * square * inverse
            head = fifth.astype(BF16)
            tail = (fifth - head.astype(F32)).astype(BF16)
            acc_ref[:, to] += jnp.dot(weights, head, preferred_element_type=F32) + jnp.dot(
                weights, tail, preferred_element_type=F32
            )


def induce(
    pos_ref, vel_ref, app_ref, sus_ref, own_ref, part_ref,
    mom_ref, pos_cols, vel_cols, mom_cols, own_back, part_back,
    block_ref, block_all, first_ref, first_all, second_ref, rows_ref, weights_ref, target_ref, acc_ref,
    row_send, row_recv, one_send, one_recv, col_send, col_recv, two_send, two_recv, local_sem,
):
    length = pos_ref.shape[1]
    half = length // 2
    parts = block_all.shape[0]
    here = lax.axis_index("row")
    column = lax.axis_index("col")

    pos = pos_ref[...] - CENTRE
    start = sus_ref[...] * app_ref[...]
    block_ref[0:3, :] = pos
    block_ref[3:6, :] = start
    target_ref[...] = target_rows(pos)
    acc_ref[...] = jnp.zeros_like(acc_ref)
    enter()

    def row_copy(source, gathered, send, recv, step):
        to = row_steps(step)[0]
        return pltpu.make_async_remote_copy(
            src_ref=source, dst_ref=gathered.at[here], send_sem=send.at[step], recv_sem=recv.at[step],
            device_id={"row": to}, device_id_type=MESH,
        )

    def row_arrival(source, gathered, send, recv, step):
        to, origin = row_steps(step)
        return pltpu.make_async_remote_copy(
            src_ref=source, dst_ref=gathered.at[origin], send_sem=send.at[step], recv_sem=recv.at[step],
            device_id={"row": to}, device_id_type=MESH,
        )

    row_args = (block_ref, block_all, row_send, row_recv)
    one_args = (first_ref, first_all, one_send, one_recv)
    each_step("row", lambda step: row_copy(*row_args, step).start())

    def col_pairs(to, origin):
        return (
            (pos_ref, pos_cols.at[:, origin, :]),
            (vel_ref, vel_cols.at[:, origin, :]),
            (own_ref.at[pl.ds(to, 1)], own_back.at[pl.ds(origin, 1)]),
            (part_ref.at[pl.ds(to, 1)], part_back.at[pl.ds(origin, 1)]),
        )

    def col_copies(to, origin, step):
        return [
            pltpu.make_async_remote_copy(
                src_ref=source, dst_ref=target, send_sem=col_send.at[k, step], recv_sem=col_recv.at[k, step],
                device_id={"col": to}, device_id_type=MESH,
            )
            for k, (source, target) in enumerate(col_pairs(to, origin))
        ]

    def col_start(step):
        for copy in col_copies(col_steps(step)[0], column, step):
            copy.start()

    def own_copies():
        return [
            pltpu.make_async_copy(source, target, local_sem.at[k])
            for k, (source, target) in enumerate(col_pairs(column, column))
        ]

    def two_copy(part, to, origin, step):
        return pltpu.make_async_remote_copy(
            src_ref=second_ref.at[part], dst_ref=mom_cols.at[part, :, origin, :],
            send_sem=two_send.at[part, step], recv_sem=two_recv.at[part, step],
            device_id={"col": to}, device_id_type=MESH,
        )

    def two_own(part):
        return pltpu.make_async_copy(second_ref.at[part], mom_cols.at[part, :, column, :], local_sem.at[4 + part])

    def two_start(part):
        each_step("col", lambda step: two_copy(part, col_steps(step)[0], column, step).start())
        two_own(part).start()

    def prepare(step, pos, mom, with_rows):
        at = pl.ds(pl.multiple_of(step * length, length), length)
        if with_rows:
            rows_ref[:, at] = source_rows(pos)
        weights_ref[:, at] = source_weights(pos, mom)

    prepare(0, pos, start, True)

    @pl.loop(0, parts)
    def _(step):
        @pl.when(step > 0)
        def _():
            row_arrival(*row_args, step).wait_recv()
            origin = row_steps(step)[1]
            prepare(step, block_all[origin, 0:3, :], block_all[origin, 3:6, :], True)

        @pl.when(step == 4)
        def _():
            each_step("col", col_start)
            for copy in own_copies():
                copy.start()

        add_field(rows_ref, weights_ref, target_ref, acc_ref, step * length, length, (0, length))

    field = combine(acc_ref[...], pos)
    first = sus_ref[...] * (app_ref[...] + (field + start))
    first_ref[...] = first
    prepare(0, pos, first, False)
    acc_ref[...] = jnp.zeros_like(acc_ref)
    each_step("row", lambda step: row_copy(*one_args, step).start())

    def finish(part):
        at = slice(part * half, part * half + half)
        field = combine(acc_ref[:, at], pos_ref[:, at] - CENTRE)
        second = sus_ref[:, at] * (app_ref[:, at] + (field + first_ref[:, at]))
        second_ref[part] = second
        mom_ref[:, at] = second

    @pl.loop(0, parts)
    def _(step):
        @pl.when(step > 0)
        def _():
            row_arrival(*one_args, step).wait_recv()
            origin = row_steps(step)[1]
            prepare(step, block_all[origin, 0:3, :], first_all[origin], False)

        add_field(rows_ref, weights_ref, target_ref, acc_ref, step * length, length, (0, half))

    finish(0)

    @pl.loop(0, parts // 2)
    def _(step):
        @pl.when(step == 1)
        def _():
            two_start(0)

        add_field(rows_ref, weights_ref, target_ref, acc_ref, step * 2 * length, 2 * length, (half, length))

    finish(1)

    def row_done(step):
        row_copy(*row_args, step).wait_send()
        row_copy(*one_args, step).wait_send()

    each_step("row", row_done)
    two_start(1)

    def col_done(step):
        to, origin = col_steps(step)
        for copy in col_copies(to, origin, step):
            copy.wait()

    each_step("col", col_done)
    for copy in own_copies():
        copy.wait()
    for part in range(2):
        each_step("col", lambda step: two_copy(part, *col_steps(step), step).wait())
        two_own(part).wait()


def picked(table, high, low):
    out = None
    for group, row in enumerate(table):
        found = jnp.take_along_axis(row, low, axis=1)
        out = found if out is None else jnp.where(high == group, found, out)
    return out


def pair_force(mine, other):
    sep = [mine[k] - other[k] for k in range(3)]
    vel = [mine[3 + k] - other[3 + k] for k in range(3)]
    m_one = mine[6:9]
    m_two = other[6:9]

    def dot(a, b):
        return a[0] * b[0] + a[1] * b[1] + a[2] * b[2]

    radius_sq = dot(sep, sep) + 1.0
    inverse = lax.rsqrt(radius_sq)
    distance = radius_sq * inverse
    normal = [s * inverse for s in sep]
    one = dot(m_one, normal)
    two = dot(m_two, normal)
    radial = 3.0 * (dot(m_one, m_two) - 5.0 * one * two)
    radial = radial - 0.03 * (distance - 1.0) - 0.5 * dot(vel, normal)
    return [3.0 * (one * m_two[k] + two * m_one[k]) + radial * normal[k] for k in range(3)]


def contact_kernel(
    pos_ref, vel_ref, mom_ref, pos_cols, vel_cols, mom_cols, own_ref, part_ref, own_back, part_back, out_ref, acc_ref
):
    columns = pos_cols.shape[1]
    length = pos_ref.shape[1]
    half = length // 2
    chunks = own_ref.shape[1] // 128
    acc_ref[...] = jnp.zeros_like(acc_ref)
    group_ids = lax.broadcasted_iota(jnp.int32, (8, 128), 0)
    lane_ids = lax.broadcasted_iota(jnp.int32, (128, 128), 0)
    groups = [slice(g * 128, g * 128 + 128) for g in range(length // 128)]

    def slots(my_ids, other_ids, live, eight):
        my_high, my_low = my_ids >> 7, my_ids & 127
        other_high, other_low = other_ids >> 7, other_ids & 127
        mine, other = [], []
        for k in range(9):
            if k < 6:
                near, far = (pos_ref, pos_cols) if k < 3 else (vel_ref, vel_cols)
                j = k % 3
                theirs = [far[j, eight, g] for g in groups]
            else:
                near, j = mom_ref, k - 6
                theirs = [mom_cols[g.start // half, j, eight, g.start % half : g.start % half + 128] for g in groups]
            ours = [jnp.broadcast_to(near[j : j + 1, g], (8, 128)) for g in groups]
            mine.append(picked(ours, my_high, my_low))
            other.append(picked(theirs, other_high, other_low))
        force = [jnp.where(live, f, 0.0) for f in pair_force(mine, other)]
        split = [p for f in force for p in pieces(f, 3)]
        left, right = [], []
        for k in range(8):
            hit = jnp.broadcast_to(my_high[k : k + 1], (8, 128)) == group_ids
            left.append(
                jnp.concatenate(
                    [jnp.where(hit, jnp.broadcast_to(p[k : k + 1], (8, 128)), 0.0) for p in split], axis=0
                ).astype(BF16)
            )
            same = jnp.broadcast_to(my_low[k : k + 1], (128, 128)) == lane_ids
            right.append(jnp.where(same, 1.0, 0.0).astype(BF16))
        acc_ref[...] += lax.dot_general(
            jnp.concatenate(left, axis=1),
            jnp.concatenate(right, axis=1),
            (((1,), (1,)), ((), ())),
            preferred_element_type=F32,
        )

    @pl.loop(0, columns // 8 * chunks)
    def _(unit):
        eight = pl.ds(pl.multiple_of(lax.div(unit, chunks) * 8, 8), 8)
        at = pl.ds(pl.multiple_of(lax.rem(unit, chunks) * 128, 128), 128)
        owner, partner = own_ref[eight, at], part_ref[eight, at]
        slots(owner, partner, owner >= 0, eight)
        owner, partner = own_back[eight, at], part_back[eight, at]
        slots(partner, owner, owner >= 0, eight)

    for k in range(3):
        base = 24 * k
        total = acc_ref[base : base + 8] + (acc_ref[base + 8 : base + 16] + acc_ref[base + 16 : base + 24])
        for g in range(8):
            out_ref[k : k + 1, g * 128 : g * 128 + 128] = total[g : g + 1]


def on_device(positions, velocity, applied, suscept, contact_owner, contact_partner, contact_count):
    rows = lax.axis_size("row")
    cols = lax.axis_size("col")
    length = positions.shape[1]
    slots = contact_owner.shape[3]
    live = jnp.arange(slots, dtype=jnp.int32)[None, :] < contact_count.reshape(cols, 1)
    owners = jnp.where(live, contact_owner.reshape(cols, slots), -1)
    partners = contact_partner.reshape(cols, slots)
    copies = pltpu.SemaphoreType.DMA
    vector = jax.ShapeDtypeStruct((3, length), F32)
    per_column = jax.ShapeDtypeStruct((3, cols, length), F32)
    moments, pos_cols, vel_cols, mom_cols, own_back, part_back = pl.pallas_call(
        induce,
        out_shape=(
            vector,
            per_column,
            per_column,
            jax.ShapeDtypeStruct((2, 3, cols, length // 2), F32),
            jax.ShapeDtypeStruct((cols, slots), jnp.int32),
            jax.ShapeDtypeStruct((cols, slots), jnp.int32),
        ),
        in_specs=vmem_specs(6),
        out_specs=tuple(vmem_specs(6)),
        scratch_shapes=[
            pltpu.VMEM((6, length), F32),
            pltpu.VMEM((rows, 6, length), F32),
            pltpu.VMEM((3, length), F32),
            pltpu.VMEM((rows, 3, length), F32),
            pltpu.VMEM((2, 3, length // 2), F32),
            pltpu.VMEM((24, rows * length), BF16),
            pltpu.VMEM((54, rows * length), BF16),
            pltpu.VMEM((24, length), BF16),
            pltpu.VMEM((54, length), F32),
            copies((rows,)), copies((rows,)), copies((rows,)), copies((rows,)),
            copies((4, cols)), copies((4, cols)), copies((2, cols)), copies((2, cols)),
            copies((6,)),
        ],
        compiler_params=pltpu.CompilerParams(collective_id=0, has_side_effects=True),
        name="induce",
    )(positions, velocity, applied, suscept.reshape(1, length), owners, partners)
    forces = pl.pallas_call(
        contact_kernel,
        out_shape=vector,
        in_specs=vmem_specs(10),
        out_specs=pl.BlockSpec(memory_space=pltpu.VMEM),
        scratch_shapes=[pltpu.VMEM((72, 128), F32)],
        name="contacts",
    )(positions, velocity, moments, pos_cols, vel_cols, mom_cols, owners, partners, own_back, part_back)
    return (moments, forces)


def solution(mesh):
    placed = (
        P(None, ("col", "row")),
        P(None, ("col", "row")),
        P(None, ("col", "row")),
        P(("col", "row")),
        P("col", "row", None, None),
        P("col", "row", None, None),
        P("col", "row", None),
    )
    return jax.shard_map(
        on_device,
        mesh=mesh,
        in_specs=placed,
        out_specs=(P(None, ("col", "row")), P(None, ("col", "row"))),
        check_vma=False,
    )
```

```python
import functools

import jax
import jax.numpy as jnp
from jax import lax
from jax.experimental import pallas as pl
from jax.experimental.pallas import tpu as pltpu
from jax.sharding import PartitionSpec as P

F32 = jnp.float32
BF16 = jnp.bfloat16
MESH = pl.DeviceIdType.MESH
CENTRE = 8.0
SRC_BLOCK = 512
ROW_SHAPE = (2, 4, 2)
KEPT = 14
TGT_BLOCK = 256


def vmem_specs(count):
    return [pl.BlockSpec(memory_space=pltpu.VMEM)] * count


def row_steps(step):
    depth, height, cores = ROW_SHAPE
    me = lax.axis_index("row")
    core, rest = lax.rem(me, cores), lax.div(me, cores)
    y, z = lax.rem(rest, height), lax.div(rest, height)
    core_by, rest_by = lax.rem(step, cores), lax.div(step, cores)
    turn, z_by = lax.rem(rest_by, height), lax.div(rest_by, height)
    y_by = turn + lax.div(turn, 2) - 2 * lax.div(turn, 3)

    def at(sign):
        new_z = lax.rem(z + depth + sign * z_by, depth)
        new_y = lax.rem(y + height + sign * y_by, height)
        new_core = lax.rem(core + cores + sign * core_by, cores)
        return (new_z * height + new_y) * cores + new_core

    return at(1), at(-1)


def col_steps(step):
    size = lax.axis_size("col")
    me = lax.axis_index("col")
    return lax.rem(me + step, size), lax.rem(me + size - step, size)


def each_step(axis, body):
    lax.fori_loop(1, lax.axis_size(axis), lambda step, carry: (body(step), carry)[1], 0)


def enter():
    barrier = pltpu.get_barrier_semaphore()

    def signal_row(step):
        pl.semaphore_signal(barrier, inc=1, device_id={"row": row_steps(step)[0]}, device_id_type=MESH)

    def signal_col(step):
        pl.semaphore_signal(barrier, inc=1, device_id={"col": col_steps(step)[0]}, device_id_type=MESH)

    each_step("row", signal_row)
    each_step("col", signal_col)


def pieces(value, count):
    out = []
    for unused in range(count):
        head = value.astype(BF16)
        wide = head.astype(F32)
        out.append(wide)
        value = value - wide
    return out


def target_rows(pos):
    first, second, third = pieces(-2.0 * pos, 3)
    norm = jnp.sum(pos * pos, axis=0, keepdims=True) + 1.0
    one = jnp.ones_like(norm)
    rows = [first, second, third, first, second, first, one, one, one] + pieces(norm, 3)
    return jnp.concatenate(rows, axis=0).astype(BF16)


def source_rows(pos):
    first, second, third = pieces(pos, 3)
    norm = jnp.sum(pos * pos, axis=0, keepdims=True)
    one = jnp.ones_like(norm)
    rows = [first, first, first, second, second, third] + pieces(norm, 3) + [one, one, one]
    return jnp.concatenate(rows, axis=0).astype(BF16)


def source_weights(pos, mom):
    norm = jnp.sum(pos * pos, axis=0, keepdims=True)
    along = jnp.sum(pos * mom, axis=0, keepdims=True)
    terms = jnp.concatenate(
        [mom, pos[0:1] * mom, pos[1:2] * mom, pos[2:3] * mom, 3.0 * (along * pos) - norm * mom], axis=0
    )
    return jnp.concatenate(pieces(terms, 3), axis=0).astype(BF16)


def combine(acc, pos):
    sums = acc[0:15] + (acc[15:30] + acc[30:45])
    x, y, z = pos[0:1], pos[1:2], pos[2:3]
    mom = sums[0:3]
    by_x, by_y, by_z = sums[3:6], sums[6:9], sums[9:12]
    mixed = sums[12:15]
    inner = x * mom[0:1] + y * mom[1:2] + z * mom[2:3]
    trace = by_x[0:1] + by_y[1:2] + by_z[2:3]
    crossed = jnp.concatenate(
        [x * by[0:1] + y * by[1:2] + z * by[2:3] for by in (by_x, by_y, by_z)], axis=0
    )
    radial = pos * (inner - trace) - crossed
    norm = jnp.sum(pos * pos, axis=0, keepdims=True) + 1.0
    direct = norm * mom - 2.0 * (x * by_x + y * by_y + z * by_z)
    return 3.0 * radial - direct + mixed


def add_sums(weights, head, tail, acc_ref, to):
    acc_ref[:, to] += jnp.dot(weights, head, preferred_element_type=F32) + jnp.dot(
        weights, tail, preferred_element_type=F32
    )


def add_field(rows_ref, weights_ref, target_ref, acc_ref, first, count, targets, kept=None):
    for start in range(0, count, SRC_BLOCK):
        at = pl.ds(pl.multiple_of(first + start, SRC_BLOCK), SRC_BLOCK)
        rows = rows_ref[:, at]
        weights = weights_ref[:, at]
        for low in range(targets[0], targets[1], TGT_BLOCK):
            to = slice(low, low + TGT_BLOCK)
            radius_sq = lax.dot_general(
                rows, target_ref[:, to], (((0,), (0,)), ((), ())), preferred_element_type=F32
            )
            inverse = lax.rsqrt(radius_sq)
            square = inverse * inverse
            fifth = square * square * inverse
            head = fifth.astype(BF16)
            tail = (fifth - head.astype(F32)).astype(BF16)
            if kept is not None:
                kept[0][at, to] = head
                kept[1][at, to] = tail
            add_sums(weights, head, tail, acc_ref, to)


def add_kept(kept, weights_ref, acc_ref, first, count, targets):
    at = pl.ds(pl.multiple_of(first, count), count)
    weights = weights_ref[:, at]
    for low in range(targets[0], targets[1], TGT_BLOCK):
        to = slice(low, low + TGT_BLOCK)
        add_sums(weights, kept[0][at, to], kept[1][at, to], acc_ref, to)


def induce(
    pos_ref, vel_ref, app_ref, sus_ref, own_ref, part_ref,
    mom_ref, pos_cols, vel_cols, mom_cols, own_back, part_back,
    block_ref, block_all, first_ref, first_all, second_ref, rows_ref, weights_ref, target_ref, acc_ref, heads, tails,
    row_send, row_recv, one_send, one_recv, col_send, col_recv, two_send, two_recv, local_sem,
):
    length = pos_ref.shape[1]
    half = length // 2
    parts = block_all.shape[0]
    here = lax.axis_index("row")
    column = lax.axis_index("col")

    enter()
    pos = pos_ref[...] - CENTRE
    start = sus_ref[...] * app_ref[...]
    block_ref[0:3, :] = pos
    block_ref[3:6, :] = start
    target_ref[...] = target_rows(pos)
    acc_ref[...] = jnp.zeros_like(acc_ref)
    kept = (heads, tails)

    def row_copy(source, gathered, send, recv, step):
        to = row_steps(step)[0]
        return pltpu.make_async_remote_copy(
            src_ref=source, dst_ref=gathered.at[here], send_sem=send.at[step], recv_sem=recv.at[step],
            device_id={"row": to}, device_id_type=MESH,
        )

    def row_arrival(source, gathered, send, recv, step):
        to, origin = row_steps(step)
        return pltpu.make_async_remote_copy(
            src_ref=source, dst_ref=gathered.at[origin], send_sem=send.at[step], recv_sem=recv.at[step],
            device_id={"row": to}, device_id_type=MESH,
        )

    row_args = (block_ref, block_all, row_send, row_recv)
    one_args = (first_ref, first_all, one_send, one_recv)
    def col_pairs(to, origin):
        return (
            (pos_ref, pos_cols.at[:, origin, :]),
            (vel_ref, vel_cols.at[:, origin, :]),
            (own_ref.at[pl.ds(to, 1)], own_back.at[pl.ds(origin, 1)]),
            (part_ref.at[pl.ds(to, 1)], part_back.at[pl.ds(origin, 1)]),
        )

    def col_copies(to, origin, step):
        return [
            pltpu.make_async_remote_copy(
                src_ref=source, dst_ref=target, send_sem=col_send.at[k, step], recv_sem=col_recv.at[k, step],
                device_id={"col": to}, device_id_type=MESH,
            )
            for k, (source, target) in enumerate(col_pairs(to, origin))
        ]

    def col_start(step):
        for copy in col_copies(col_steps(step)[0], column, step):
            copy.start()

    def own_copies():
        return [
            pltpu.make_async_copy(source, target, local_sem.at[k])
            for k, (source, target) in enumerate(col_pairs(column, column))
        ]

    def two_copy(part, to, origin, step):
        return pltpu.make_async_remote_copy(
            src_ref=second_ref.at[part], dst_ref=mom_cols.at[part, :, origin, :],
            send_sem=two_send.at[part, step], recv_sem=two_recv.at[part, step],
            device_id={"col": to}, device_id_type=MESH,
        )

    def two_own(part):
        return pltpu.make_async_copy(second_ref.at[part], mom_cols.at[part, :, column, :], local_sem.at[4 + part])

    def two_start(part):
        each_step("col", lambda step: two_copy(part, col_steps(step)[0], column, step).start())
        two_own(part).start()

    def prepare(step, pos, mom, with_rows):
        at = pl.ds(pl.multiple_of(step * length, length), length)
        if with_rows:
            rows_ref[:, at] = source_rows(pos)
        weights_ref[:, at] = source_weights(pos, mom)

    prepare(0, pos, start, True)
    pl.semaphore_wait(pltpu.get_barrier_semaphore(), lax.axis_size("row") + lax.axis_size("col") - 2)
    each_step("row", lambda step: row_copy(*row_args, step).start())

    def take_first(step):
        row_arrival(*row_args, step).wait_recv()
        origin = row_steps(step)[1]
        prepare(step, block_all[origin, 0:3, :], block_all[origin, 3:6, :], True)

    @pl.loop(0, KEPT)
    def _(step):
        @pl.when(step > 0)
        def _():
            take_first(step)

        @pl.when(step == 4)
        def _():
            each_step("col", col_start)
            for copy in own_copies():
                copy.start()

        add_field(rows_ref, weights_ref, target_ref, acc_ref, step * length, length, (0, length), kept)

    @pl.loop(KEPT, parts)
    def _(step):
        take_first(step)
        add_field(rows_ref, weights_ref, target_ref, acc_ref, step * length, length, (0, length))

    field = combine(acc_ref[...], pos)
    first = sus_ref[...] * (app_ref[...] + (field + start))
    first_ref[...] = first
    prepare(0, pos, first, False)
    acc_ref[...] = jnp.zeros_like(acc_ref)
    each_step("row", lambda step: row_copy(*one_args, step).start())

    def finish(part):
        at = slice(part * half, part * half + half)
        field = combine(acc_ref[:, at], pos_ref[:, at] - CENTRE)
        second = sus_ref[:, at] * (app_ref[:, at] + (field + first_ref[:, at]))
        second_ref[part] = second
        mom_ref[:, at] = second

    def take_second(step):
        row_arrival(*one_args, step).wait_recv()
        origin = row_steps(step)[1]
        prepare(step, block_all[origin, 0:3, :], first_all[origin], False)

    @pl.loop(0, KEPT)
    def _(step):
        @pl.when(step > 0)
        def _():
            take_second(step)

        add_kept(kept, weights_ref, acc_ref, step * length, length, (0, half))

    @pl.loop(KEPT, parts)
    def _(step):
        take_second(step)
        add_field(rows_ref, weights_ref, target_ref, acc_ref, step * length, length, (0, half))

    finish(0)

    @pl.loop(0, KEPT // 2)
    def _(step):
        @pl.when(step == 1)
        def _():
            two_start(0)

        add_kept(kept, weights_ref, acc_ref, step * 2 * length, 2 * length, (half, length))

    add_field(rows_ref, weights_ref, target_ref, acc_ref, KEPT * length, (parts - KEPT) * length, (half, length))
    finish(1)

    def row_done(step):
        row_copy(*row_args, step).wait_send()
        row_copy(*one_args, step).wait_send()

    each_step("row", row_done)
    two_start(1)

    def col_done(step):
        to, origin = col_steps(step)
        for copy in col_copies(to, origin, step):
            copy.wait()

    each_step("col", col_done)
    for copy in own_copies():
        copy.wait()
    for part in range(2):
        each_step("col", lambda step: two_copy(part, *col_steps(step), step).wait())
        two_own(part).wait()


def picked(table, high, low):
    out = None
    for group, row in enumerate(table):
        found = jnp.take_along_axis(row, low, axis=1)
        out = found if out is None else jnp.where(high == group, found, out)
    return out


def pair_force(mine, other):
    sep = [mine[k] - other[k] for k in range(3)]
    vel = [mine[3 + k] - other[3 + k] for k in range(3)]
    m_one = mine[6:9]
    m_two = other[6:9]

    def dot(a, b):
        return a[0] * b[0] + a[1] * b[1] + a[2] * b[2]

    radius_sq = dot(sep, sep) + 1.0
    inverse = lax.rsqrt(radius_sq)
    distance = radius_sq * inverse
    normal = [s * inverse for s in sep]
    one = dot(m_one, normal)
    two = dot(m_two, normal)
    radial = 3.0 * (dot(m_one, m_two) - 5.0 * one * two)
    radial = radial - 0.03 * (distance - 1.0) - 0.5 * dot(vel, normal)
    return [3.0 * (one * m_two[k] + two * m_one[k]) + radial * normal[k] for k in range(3)]


def contact_kernel(
    pos_ref, vel_ref, mom_ref, pos_cols, vel_cols, mom_cols, own_ref, part_ref, own_back, part_back, out_ref, acc_ref
):
    columns = pos_cols.shape[1]
    length = pos_ref.shape[1]
    half = length // 2
    chunks = own_ref.shape[1] // 128
    acc_ref[...] = jnp.zeros_like(acc_ref)
    group_ids = lax.broadcasted_iota(jnp.int32, (8, 128), 0)
    lane_ids = lax.broadcasted_iota(jnp.int32, (128, 128), 0)
    groups = [slice(g * 128, g * 128 + 128) for g in range(length // 128)]

    def slots(my_ids, other_ids, live, eight):
        my_high, my_low = my_ids >> 7, my_ids & 127
        other_high, other_low = other_ids >> 7, other_ids & 127
        mine, other = [], []
        for k in range(9):
            if k < 6:
                near, far = (pos_ref, pos_cols) if k < 3 else (vel_ref, vel_cols)
                j = k % 3
                theirs = [far[j, eight, g] for g in groups]
            else:
                near, j = mom_ref, k - 6
                theirs = [mom_cols[g.start // half, j, eight, g.start % half : g.start % half + 128] for g in groups]
            ours = [jnp.broadcast_to(near[j : j + 1, g], (8, 128)) for g in groups]
            mine.append(picked(ours, my_high, my_low))
            other.append(picked(theirs, other_high, other_low))
        force = [jnp.where(live, f, 0.0) for f in pair_force(mine, other)]
        split = [p for f in force for p in pieces(f, 3)]
        left, right = [], []
        for k in range(8):
            hit = jnp.broadcast_to(my_high[k : k + 1], (8, 128)) == group_ids
            left.append(
                jnp.concatenate(
                    [jnp.where(hit, jnp.broadcast_to(p[k : k + 1], (8, 128)), 0.0) for p in split], axis=0
                ).astype(BF16)
            )
            same = jnp.broadcast_to(my_low[k : k + 1], (128, 128)) == lane_ids
            right.append(jnp.where(same, 1.0, 0.0).astype(BF16))
        acc_ref[...] += lax.dot_general(
            jnp.concatenate(left, axis=1),
            jnp.concatenate(right, axis=1),
            (((1,), (1,)), ((), ())),
            preferred_element_type=F32,
        )

    @pl.loop(0, columns // 8 * chunks)
    def _(unit):
        eight = pl.ds(pl.multiple_of(lax.div(unit, chunks) * 8, 8), 8)
        at = pl.ds(pl.multiple_of(lax.rem(unit, chunks) * 128, 128), 128)
        owner, partner = own_ref[eight, at], part_ref[eight, at]
        slots(owner, partner, owner >= 0, eight)
        owner, partner = own_back[eight, at], part_back[eight, at]
        slots(partner, owner, owner >= 0, eight)

    for k in range(3):
        base = 24 * k
        total = acc_ref[base : base + 8] + (acc_ref[base + 8 : base + 16] + acc_ref[base + 16 : base + 24])
        for g in range(8):
            out_ref[k : k + 1, g * 128 : g * 128 + 128] = total[g : g + 1]


def on_device(positions, velocity, applied, suscept, contact_owner, contact_partner, contact_count):
    rows = lax.axis_size("row")
    cols = lax.axis_size("col")
    length = positions.shape[1]
    slots = contact_owner.shape[3]
    live = jnp.arange(slots, dtype=jnp.int32)[None, :] < contact_count.reshape(cols, 1)
    owners = jnp.where(live, contact_owner.reshape(cols, slots), -1)
    partners = contact_partner.reshape(cols, slots)
    copies = pltpu.SemaphoreType.DMA
    vector = jax.ShapeDtypeStruct((3, length), F32)
    per_column = jax.ShapeDtypeStruct((3, cols, length), F32)
    moments, pos_cols, vel_cols, mom_cols, own_back, part_back = pl.pallas_call(
        induce,
        out_shape=(
            vector,
            per_column,
            per_column,
            jax.ShapeDtypeStruct((2, 3, cols, length // 2), F32),
            jax.ShapeDtypeStruct((cols, slots), jnp.int32),
            jax.ShapeDtypeStruct((cols, slots), jnp.int32),
        ),
        in_specs=vmem_specs(6),
        out_specs=tuple(vmem_specs(6)),
        scratch_shapes=[
            pltpu.VMEM((6, length), F32),
            pltpu.VMEM((rows, 6, length), F32),
            pltpu.VMEM((3, length), F32),
            pltpu.VMEM((rows, 3, length), F32),
            pltpu.VMEM((2, 3, length // 2), F32),
            pltpu.VMEM((24, rows * length), BF16),
            pltpu.VMEM((45, rows * length), BF16),
            pltpu.VMEM((24, length), BF16),
            pltpu.VMEM((45, length), F32),
            pltpu.VMEM((KEPT * length, length), BF16),
            pltpu.VMEM((KEPT * length, length), BF16),
            copies((rows,)), copies((rows,)), copies((rows,)), copies((rows,)),
            copies((4, cols)), copies((4, cols)), copies((2, cols)), copies((2, cols)),
            copies((6,)),
        ],
        compiler_params=pltpu.CompilerParams(
            collective_id=0, has_side_effects=True, vmem_limit_bytes=67043328
        ),
        name="induce",
    )(positions, velocity, applied, suscept.reshape(1, length), owners, partners)
    forces = pl.pallas_call(
        contact_kernel,
        out_shape=vector,
        in_specs=vmem_specs(10),
        out_specs=pl.BlockSpec(memory_space=pltpu.VMEM),
        scratch_shapes=[pltpu.VMEM((72, 128), F32)],
        name="contacts",
    )(positions, velocity, moments, pos_cols, vel_cols, mom_cols, owners, partners, own_back, part_back)
    return (moments, forces)


def solution(mesh):
    placed = (
        P(None, ("col", "row")),
        P(None, ("col", "row")),
        P(None, ("col", "row")),
        P(("col", "row")),
        P("col", "row", None, None),
        P("col", "row", None, None),
        P("col", "row", None),
    )
    return jax.shard_map(
        on_device,
        mesh=mesh,
        in_specs=placed,
        out_specs=(P(None, ("col", "row")), P(None, ("col", "row"))),
        check_vma=False,
    )
```

```python
import functools

import jax
import jax.numpy as jnp
from jax import lax
from jax.experimental import pallas as pl
from jax.experimental.pallas import tpu as pltpu
from jax.sharding import PartitionSpec as P

F32 = jnp.float32
BF16 = jnp.bfloat16
MESH = pl.DeviceIdType.MESH
CENTRE = 8.0
SRC_BLOCK = 512
ROW_SHAPE = (2, 4, 2)
KEPT = 14
TGT_BLOCK = 256


def vmem_specs(count):
    return [pl.BlockSpec(memory_space=pltpu.VMEM)] * count


def row_steps(step):
    depth, height, cores = ROW_SHAPE
    me = lax.axis_index("row")
    core, rest = lax.rem(me, cores), lax.div(me, cores)
    y, z = lax.rem(rest, height), lax.div(rest, height)
    core_by, rest_by = lax.rem(step, cores), lax.div(step, cores)
    turn, z_by = lax.rem(rest_by, height), lax.div(rest_by, height)
    y_by = turn + lax.div(turn, 2) - 2 * lax.div(turn, 3)

    def at(sign):
        new_z = lax.rem(z + depth + sign * z_by, depth)
        new_y = lax.rem(y + height + sign * y_by, height)
        new_core = lax.rem(core + cores + sign * core_by, cores)
        return (new_z * height + new_y) * cores + new_core

    return at(1), at(-1)


def col_steps(step):
    size = lax.axis_size("col")
    me = lax.axis_index("col")
    return lax.rem(me + step, size), lax.rem(me + size - step, size)


def each_step(axis, body):
    lax.fori_loop(1, lax.axis_size(axis), lambda step, carry: (body(step), carry)[1], 0)


def enter():
    barrier = pltpu.get_barrier_semaphore()

    def signal_row(step):
        pl.semaphore_signal(barrier, inc=1, device_id={"row": row_steps(step)[0]}, device_id_type=MESH)

    def signal_col(step):
        pl.semaphore_signal(barrier, inc=1, device_id={"col": col_steps(step)[0]}, device_id_type=MESH)

    each_step("row", signal_row)
    each_step("col", signal_col)


def pieces(value, count):
    out = []
    for unused in range(count):
        head = value.astype(BF16)
        wide = head.astype(F32)
        out.append(wide)
        value = value - wide
    return out


def target_rows(pos):
    first, second, third = pieces(-2.0 * pos, 3)
    norm = jnp.sum(pos * pos, axis=0, keepdims=True) + 1.0
    one = jnp.ones_like(norm)
    rows = [first, second, third, first, second, first, one, one, one] + pieces(norm, 3)
    return jnp.concatenate(rows, axis=0).astype(BF16)


def source_rows(pos):
    first, second, third = pieces(pos, 3)
    norm = jnp.sum(pos * pos, axis=0, keepdims=True)
    one = jnp.ones_like(norm)
    rows = [first, first, first, second, second, third] + pieces(norm, 3) + [one, one, one]
    return jnp.concatenate(rows, axis=0).astype(BF16)


def source_weights(pos, mom):
    norm = jnp.sum(pos * pos, axis=0, keepdims=True)
    along = jnp.sum(pos * mom, axis=0, keepdims=True)
    terms = jnp.concatenate(
        [mom, pos[0:1] * mom, pos[1:2] * mom, pos[2:3] * mom, 3.0 * (along * pos) - norm * mom], axis=0
    )
    return jnp.concatenate(pieces(terms, 3), axis=0).astype(BF16)


def combine(acc, pos):
    sums = acc[0:15] + (acc[15:30] + acc[30:45])
    x, y, z = pos[0:1], pos[1:2], pos[2:3]
    mom = sums[0:3]
    by_x, by_y, by_z = sums[3:6], sums[6:9], sums[9:12]
    mixed = sums[12:15]
    inner = x * mom[0:1] + y * mom[1:2] + z * mom[2:3]
    trace = by_x[0:1] + by_y[1:2] + by_z[2:3]
    crossed = jnp.concatenate(
        [x * by[0:1] + y * by[1:2] + z * by[2:3] for by in (by_x, by_y, by_z)], axis=0
    )
    radial = pos * (inner - trace) - crossed
    norm = jnp.sum(pos * pos, axis=0, keepdims=True) + 1.0
    direct = norm * mom - 2.0 * (x * by_x + y * by_y + z * by_z)
    return 3.0 * radial - direct + mixed


def add_sums(weights, head, tail, acc_ref, to):
    acc_ref[:, to] += jnp.dot(weights, head, preferred_element_type=F32) + jnp.dot(
        weights, tail, preferred_element_type=F32
    )


def add_field(rows_ref, weights_ref, target_ref, acc_ref, first, count, targets, kept=None):
    for start in range(0, count, SRC_BLOCK):
        at = pl.ds(pl.multiple_of(first + start, SRC_BLOCK), SRC_BLOCK)
        rows = rows_ref[:, at]
        weights = weights_ref[:, at]
        for low in range(targets[0], targets[1], TGT_BLOCK):
            to = slice(low, low + TGT_BLOCK)
            radius_sq = lax.dot_general(
                rows, target_ref[:, to], (((0,), (0,)), ((), ())), preferred_element_type=F32
            )
            inverse = lax.rsqrt(radius_sq)
            square = inverse * inverse
            fifth = square * square * inverse
            head = fifth.astype(BF16)
            tail = (fifth - head.astype(F32)).astype(BF16)
            if kept is not None:
                kept[0][at, to] = head
                kept[1][at, to] = tail
            add_sums(weights, head, tail, acc_ref, to)


def add_kept(kept, weights_ref, acc_ref, first, count, targets):
    at = pl.ds(pl.multiple_of(first, count), count)
    weights = weights_ref[:, at]
    for low in range(targets[0], targets[1], TGT_BLOCK):
        to = slice(low, low + TGT_BLOCK)
        add_sums(weights, kept[0][at, to], kept[1][at, to], acc_ref, to)


def picked(table, high, low, first=0):
    out = None
    for group, row in enumerate(table):
        found = jnp.take_along_axis(row, low, axis=1)
        out = found if out is None else jnp.where(high == first + group, found, out)
    return out


def dot3(a, b):
    return a[0] * b[0] + a[1] * b[1] + a[2] * b[2]


def geometry(mine, other, live):
    sep = [mine[k] - other[k] for k in range(3)]
    vel = [mine[3 + k] - other[3 + k] for k in range(3)]
    radius_sq = dot3(sep, sep) + 1.0
    inverse = lax.rsqrt(radius_sq)
    normal = [jnp.where(live, s * inverse, 0.0) for s in sep]
    return normal + [-0.03 * (radius_sq * inverse - 1.0) - 0.5 * dot3(vel, normal)]


def pair_force(normal, along, m_one, m_two):
    one = dot3(m_one, normal)
    two = dot3(m_two, normal)
    radial = 3.0 * (dot3(m_one, m_two) - 5.0 * one * two) + along
    return [3.0 * (one * m_two[k] + two * m_one[k]) + radial * normal[k] for k in range(3)]


def scatter_to(acc_ref, force, high, low):
    group_ids = lax.broadcasted_iota(jnp.int32, (8, 128), 0)
    lane_ids = lax.broadcasted_iota(jnp.int32, (128, 128), 0)
    split = [p for f in force for p in pieces(f, 3)]
    left, right = [], []
    for k in range(8):
        hit = jnp.broadcast_to(high[k : k + 1], (8, 128)) == group_ids
        left.append(
            jnp.concatenate(
                [jnp.where(hit, jnp.broadcast_to(p[k : k + 1], (8, 128)), 0.0) for p in split], axis=0
            ).astype(BF16)
        )
        same = jnp.broadcast_to(low[k : k + 1], (128, 128)) == lane_ids
        right.append(jnp.where(same, 1.0, 0.0).astype(BF16))
    acc_ref[...] += lax.dot_general(
        jnp.concatenate(left, axis=1),
        jnp.concatenate(right, axis=1),
        (((1,), (1,)), ((), ())),
        preferred_element_type=F32,
    )


def induce(
    pos_ref, vel_ref, app_ref, sus_ref, raw_ref, part_ref, count_ref,
    mom_ref, force_ref,
    pos_cols, vel_cols, mom_cols, own_ref, own_back, part_back, geo_ref, near_ref, far_ref, sums_ref,
    block_ref, block_all, first_ref, first_all, second_ref, rows_ref, weights_ref, target_ref, acc_ref, heads, tails,
    row_send, row_recv, one_send, one_recv, col_send, col_recv, two_send, two_recv, local_sem,
):
    length = pos_ref.shape[1]
    half = length // 2
    parts = block_all.shape[0]
    here = lax.axis_index("row")
    column = lax.axis_index("col")

    enter()
    pos = pos_ref[...] - CENTRE
    start = sus_ref[...] * app_ref[...]
    block_ref[0:3, :] = pos
    block_ref[3:6, :] = start
    target_ref[...] = target_rows(pos)
    acc_ref[...] = jnp.zeros_like(acc_ref)
    kept = (heads, tails)
    sums_ref[...] = jnp.zeros_like(sums_ref)
    columns, slots = raw_ref.shape
    on_diagonal = lax.broadcasted_iota(jnp.int32, (columns, columns), 0) == lax.broadcasted_iota(
        jnp.int32, (columns, columns), 1
    )
    counts = jnp.sum(
        jnp.where(on_diagonal, jnp.broadcast_to(count_ref[...], (columns, columns)).astype(F32), 0.0),
        axis=1, keepdims=True,
    )
    slot_ids = lax.broadcasted_iota(jnp.int32, (columns, slots), 1).astype(F32)
    own_ref[...] = jnp.where(slot_ids < counts, raw_ref[...], -1)

    def row_copy(source, gathered, send, recv, step):
        to = row_steps(step)[0]
        return pltpu.make_async_remote_copy(
            src_ref=source, dst_ref=gathered.at[here], send_sem=send.at[step], recv_sem=recv.at[step],
            device_id={"row": to}, device_id_type=MESH,
        )

    def row_arrival(source, gathered, send, recv, step):
        to, origin = row_steps(step)
        return pltpu.make_async_remote_copy(
            src_ref=source, dst_ref=gathered.at[origin], send_sem=send.at[step], recv_sem=recv.at[step],
            device_id={"row": to}, device_id_type=MESH,
        )

    row_args = (block_ref, block_all, row_send, row_recv)
    one_args = (first_ref, first_all, one_send, one_recv)
    def col_pairs(to, origin):
        return (
            (pos_ref, pos_cols.at[:, origin, :]),
            (vel_ref, vel_cols.at[:, origin, :]),
            (own_ref.at[pl.ds(to, 1)], own_back.at[pl.ds(origin, 1)]),
            (part_ref.at[pl.ds(to, 1)], part_back.at[pl.ds(origin, 1)]),
        )

    def col_copies(to, origin, step):
        return [
            pltpu.make_async_remote_copy(
                src_ref=source, dst_ref=target, send_sem=col_send.at[k, step], recv_sem=col_recv.at[k, step],
                device_id={"col": to}, device_id_type=MESH,
            )
            for k, (source, target) in enumerate(col_pairs(to, origin))
        ]

    def col_start(step):
        for copy in col_copies(col_steps(step)[0], column, step):
            copy.start()

    def own_copies():
        return [
            pltpu.make_async_copy(source, target, local_sem.at[k])
            for k, (source, target) in enumerate(col_pairs(column, column))
        ]

    def two_copy(part, to, origin, step):
        return pltpu.make_async_remote_copy(
            src_ref=second_ref.at[part], dst_ref=mom_cols.at[part, :, origin, :],
            send_sem=two_send.at[part, step], recv_sem=two_recv.at[part, step],
            device_id={"col": to}, device_id_type=MESH,
        )

    def two_own(part):
        return pltpu.make_async_copy(second_ref.at[part], mom_cols.at[part, :, column, :], local_sem.at[4 + part])

    def two_start(part):
        each_step("col", lambda step: two_copy(part, col_steps(step)[0], column, step).start())
        two_own(part).start()

    def prepare(step, pos, mom, with_rows):
        at = pl.ds(pl.multiple_of(step * length, length), length)
        if with_rows:
            rows_ref[:, at] = source_rows(pos)
        weights_ref[:, at] = source_weights(pos, mom)

    prepare(0, pos, start, True)
    pl.semaphore_wait(pltpu.get_barrier_semaphore(), lax.axis_size("row") + lax.axis_size("col") - 2)
    each_step("row", lambda step: row_copy(*row_args, step).start())

    def take_first(step):
        row_arrival(*row_args, step).wait_recv()
        origin = row_steps(step)[1]
        prepare(step, block_all[origin, 0:3, :], block_all[origin, 3:6, :], True)

    @pl.loop(0, KEPT)
    def _(step):
        @pl.when(step > 0)
        def _():
            take_first(step)

        @pl.when(step == 4)
        def _():
            each_step("col", col_start)
            for copy in own_copies():
                copy.start()

        add_field(rows_ref, weights_ref, target_ref, acc_ref, step * length, length, (0, length), kept)

    @pl.loop(KEPT, parts)
    def _(step):
        take_first(step)
        add_field(rows_ref, weights_ref, target_ref, acc_ref, step * length, length, (0, length))

    field = combine(acc_ref[...], pos)
    first = sus_ref[...] * (app_ref[...] + (field + start))
    first_ref[...] = first
    prepare(0, pos, first, False)
    acc_ref[...] = jnp.zeros_like(acc_ref)
    each_step("row", lambda step: row_copy(*one_args, step).start())

    chunks = slots // 128
    units = columns // 8 * chunks
    groups = [slice(g * 128, g * 128 + 128) for g in range(length // 128)]
    split_at = len(groups) // 2

    def lists(unit):
        eight = pl.ds(pl.multiple_of(lax.div(unit, chunks) * 8, 8), 8)
        at = pl.ds(pl.multiple_of(lax.rem(unit, chunks) * 128, 128), 128)
        here_own, here_part = own_ref[eight, at], part_ref[eight, at]
        back_own, back_part = own_back[eight, at], part_back[eight, at]
        return eight, ((here_own, here_part, here_own >= 0), (back_part, back_own, back_own >= 0))

    def spread(ref, j):
        return [jnp.broadcast_to(ref[j : j + 1, g], (8, 128)) for g in groups]

    def halves(part, j, eight):
        return [mom_cols[part, j, eight, groups[g]] for g in range(split_at)]

    def col_done(step):
        to, origin = col_steps(step)
        for copy in col_copies(to, origin, step):
            copy.wait()

    each_step("col", col_done)
    for copy in own_copies():
        copy.wait()

    @pl.loop(0, units)
    def _(unit):
        eight, both = lists(unit)
        for which, (my_ids, other_ids, live) in enumerate(both):
            mine, other = [], []
            for near, far in ((pos_ref, pos_cols), (vel_ref, vel_cols)):
                for j in range(3):
                    mine.append(picked(spread(near, j), my_ids >> 7, my_ids & 127))
                    other.append(picked([far[j, eight, g] for g in groups], other_ids >> 7, other_ids & 127))
            for k, value in enumerate(geometry(mine, other, live)):
                geo_ref[unit, which, k] = value

    def finish(part):
        at = slice(part * half, part * half + half)
        field = combine(acc_ref[:, at], pos_ref[:, at] - CENTRE)
        second = sus_ref[:, at] * (app_ref[:, at] + (field + first_ref[:, at]))
        second_ref[part] = second
        mom_ref[:, at] = second

    def take_second(step):
        row_arrival(*one_args, step).wait_recv()
        origin = row_steps(step)[1]
        prepare(step, block_all[origin, 0:3, :], first_all[origin], False)

    @pl.loop(0, KEPT)
    def _(step):
        @pl.when(step > 0)
        def _():
            take_second(step)

        add_kept(kept, weights_ref, acc_ref, step * length, length, (0, half))

    @pl.loop(KEPT, parts)
    def _(step):
        take_second(step)
        add_field(rows_ref, weights_ref, target_ref, acc_ref, step * length, length, (0, half))

    finish(0)

    @pl.loop(0, KEPT // 2)
    def _(step):
        @pl.when(step == 1)
        def _():
            two_start(0)

        add_kept(kept, weights_ref, acc_ref, step * 2 * length, 2 * length, (half, length))

    add_field(rows_ref, weights_ref, target_ref, acc_ref, KEPT * length, (parts - KEPT) * length, (half, length))
    finish(1)

    def row_done(step):
        row_copy(*row_args, step).wait_send()
        row_copy(*one_args, step).wait_send()

    each_step("row", row_done)
    two_start(1)


    def two_done(part):
        each_step("col", lambda step: two_copy(part, *col_steps(step), step).wait())
        two_own(part).wait()

    two_done(0)

    @pl.loop(0, units)
    def _(unit):
        eight, both = lists(unit)
        for which, (my_ids, other_ids, live) in enumerate(both):
            for j in range(3):
                near_ref[unit, which, j] = picked(spread(mom_ref, j), my_ids >> 7, my_ids & 127)
                far_ref[unit, which, j] = picked(halves(0, j, eight), other_ids >> 7, other_ids & 127)

    two_done(1)

    @pl.loop(0, units)
    def _(unit):
        eight, both = lists(unit)
        for which, (my_ids, other_ids, live) in enumerate(both):
            high, low = other_ids >> 7, other_ids & 127
            theirs = [
                jnp.where(high < split_at, far_ref[unit, which, j], picked(halves(1, j, eight), high, low, split_at))
                for j in range(3)
            ]
            ours = [near_ref[unit, which, j] for j in range(3)]
            normal = [geo_ref[unit, which, k] for k in range(3)]
            force = pair_force(normal, geo_ref[unit, which, 3], ours, theirs)
            scatter_to(sums_ref, force, my_ids >> 7, my_ids & 127)

    for k in range(3):
        base = 24 * k
        total = sums_ref[base : base + 8] + (sums_ref[base + 8 : base + 16] + sums_ref[base + 16 : base + 24])
        for g in range(8):
            force_ref[k : k + 1, groups[g]] = total[g : g + 1]


def on_device(positions, velocity, applied, suscept, contact_owner, contact_partner, contact_count):
    rows = lax.axis_size("row")
    cols = lax.axis_size("col")
    length = positions.shape[1]
    slots = contact_owner.shape[3]
    copies = pltpu.SemaphoreType.DMA
    vector = jax.ShapeDtypeStruct((3, length), F32)
    units = cols // 8 * (slots // 128)
    return pl.pallas_call(
        induce,
        out_shape=(vector, vector),
        in_specs=vmem_specs(7),
        out_specs=tuple(vmem_specs(2)),
        scratch_shapes=[
            pltpu.VMEM((3, cols, length), F32),
            pltpu.VMEM((3, cols, length), F32),
            pltpu.VMEM((2, 3, cols, length // 2), F32),
            pltpu.VMEM((cols, slots), jnp.int32),
            pltpu.VMEM((cols, slots), jnp.int32),
            pltpu.VMEM((cols, slots), jnp.int32),
            pltpu.VMEM((units, 2, 4, 8, 128), F32),
            pltpu.VMEM((units, 2, 3, 8, 128), F32),
            pltpu.VMEM((units, 2, 3, 8, 128), F32),
            pltpu.VMEM((72, 128), F32),
            pltpu.VMEM((6, length), F32),
            pltpu.VMEM((rows, 6, length), F32),
            pltpu.VMEM((3, length), F32),
            pltpu.VMEM((rows, 3, length), F32),
            pltpu.VMEM((2, 3, length // 2), F32),
            pltpu.VMEM((24, rows * length), BF16),
            pltpu.VMEM((45, rows * length), BF16),
            pltpu.VMEM((24, length), BF16),
            pltpu.VMEM((45, length), F32),
            pltpu.VMEM((KEPT * length, length), BF16),
            pltpu.VMEM((KEPT * length, length), BF16),
            copies((rows,)), copies((rows,)), copies((rows,)), copies((rows,)),
            copies((4, cols)), copies((4, cols)), copies((2, cols)), copies((2, cols)),
            copies((6,)),
        ],
        compiler_params=pltpu.CompilerParams(
            collective_id=0, has_side_effects=True, vmem_limit_bytes=67043328
        ),
        name="induce",
    )(
        positions, velocity, applied, suscept.reshape(1, length),
        contact_owner.reshape(cols, slots), contact_partner.reshape(cols, slots), contact_count.reshape(1, cols),
    )


def solution(mesh):
    placed = (
        P(None, ("col", "row")),
        P(None, ("col", "row")),
        P(None, ("col", "row")),
        P(("col", "row")),
        P("col", "row", None, None),
        P("col", "row", None, None),
        P("col", "row", None),
    )
    return jax.shard_map(
        on_device,
        mesh=mesh,
        in_specs=placed,
        out_specs=(P(None, ("col", "row")), P(None, ("col", "row"))),
        check_vma=False,
    )
```

```python
import functools

import jax
import jax.numpy as jnp
from jax import lax
from jax.experimental import pallas as pl
from jax.experimental.pallas import tpu as pltpu
from jax.sharding import PartitionSpec as P

F32 = jnp.float32
BF16 = jnp.bfloat16
MESH = pl.DeviceIdType.MESH
CENTRE = 8.0
SRC_BLOCK = 512
ROW_SHAPE = (2, 4, 2)
KEPT = 14
TAIL_ROWS = 32
EARLY = 4
TGT_BLOCK = 256


def vmem_specs(count):
    return [pl.BlockSpec(memory_space=pltpu.VMEM)] * count


def row_steps(step):
    depth, height, cores = ROW_SHAPE
    me = lax.axis_index("row")
    core, rest = lax.rem(me, cores), lax.div(me, cores)
    y, z = lax.rem(rest, height), lax.div(rest, height)
    core_by, rest_by = lax.rem(step, cores), lax.div(step, cores)
    turn, z_by = lax.rem(rest_by, height), lax.div(rest_by, height)
    y_by = turn + lax.div(turn, 2) - 2 * lax.div(turn, 3)

    def at(sign):
        new_z = lax.rem(z + depth + sign * z_by, depth)
        new_y = lax.rem(y + height + sign * y_by, height)
        new_core = lax.rem(core + cores + sign * core_by, cores)
        return (new_z * height + new_y) * cores + new_core

    return at(1), at(-1)


def col_steps(step):
    size = lax.axis_size("col")
    me = lax.axis_index("col")
    return lax.rem(me + step, size), lax.rem(me + size - step, size)


def each_step(axis, body):
    lax.fori_loop(1, lax.axis_size(axis), lambda step, carry: (body(step), carry)[1], 0)


def every_step(axis, body):
    for step in range(1, lax.axis_size(axis)):
        body(step)


def enter():
    barrier = pltpu.get_barrier_semaphore()

    def signal_row(step):
        pl.semaphore_signal(barrier, inc=1, device_id={"row": row_steps(step)[0]}, device_id_type=MESH)

    def signal_col(step):
        pl.semaphore_signal(barrier, inc=1, device_id={"col": col_steps(step)[0]}, device_id_type=MESH)

    every_step("row", signal_row)
    every_step("col", signal_col)


def pieces(value, count):
    out = []
    for unused in range(count):
        head = value.astype(BF16)
        wide = head.astype(F32)
        out.append(wide)
        value = value - wide
    return out


def target_rows(pos):
    first, second, third = pieces(-2.0 * pos, 3)
    norm = jnp.sum(pos * pos, axis=0, keepdims=True) + 1.0
    one = jnp.ones_like(norm)
    rows = [first, second, third, first, second, first, one, one, one] + pieces(norm, 3)
    return jnp.concatenate(rows, axis=0).astype(BF16)


def source_rows(pos):
    first, second, third = pieces(pos, 3)
    norm = jnp.sum(pos * pos, axis=0, keepdims=True)
    one = jnp.ones_like(norm)
    rows = [first, first, first, second, second, third] + pieces(norm, 3) + [one, one, one]
    return jnp.concatenate(rows, axis=0).astype(BF16)


def source_weights(pos, mom):
    norm = jnp.sum(pos * pos, axis=0, keepdims=True)
    along = jnp.sum(pos * mom, axis=0, keepdims=True)
    terms = jnp.concatenate(
        [mom, pos[0:1] * mom, pos[1:2] * mom, pos[2:3] * mom, 3.0 * (along * pos) - norm * mom], axis=0
    )
    return jnp.concatenate(pieces(terms, 3), axis=0).astype(BF16)


def combine(acc, pos):
    sums = acc[0:15] + (acc[15:30] + acc[30:45])
    x, y, z = pos[0:1], pos[1:2], pos[2:3]
    mom = sums[0:3]
    by_x, by_y, by_z = sums[3:6], sums[6:9], sums[9:12]
    mixed = sums[12:15]
    inner = x * mom[0:1] + y * mom[1:2] + z * mom[2:3]
    trace = by_x[0:1] + by_y[1:2] + by_z[2:3]
    crossed = jnp.concatenate(
        [x * by[0:1] + y * by[1:2] + z * by[2:3] for by in (by_x, by_y, by_z)], axis=0
    )
    radial = pos * (inner - trace) - crossed
    norm = jnp.sum(pos * pos, axis=0, keepdims=True) + 1.0
    direct = norm * mom - 2.0 * (x * by_x + y * by_y + z * by_z)
    return 3.0 * radial - direct + mixed


def span(start, size):
    return pl.ds(start if isinstance(start, int) else pl.multiple_of(start, size), size)


def add_sums(weights, head, tail, acc_ref, to):
    acc_ref[:, to] += jnp.dot(weights, head, preferred_element_type=F32)
    acc_ref[0:TAIL_ROWS, to] += jnp.dot(weights[0:TAIL_ROWS], tail, preferred_element_type=F32)


def add_field(rows_ref, weights_ref, target_ref, acc_ref, first, count, targets, kept=None):
    for start in range(0, count, SRC_BLOCK):
        at = span(first + start, SRC_BLOCK)
        rows = rows_ref[:, at]
        weights = weights_ref[:, at]
        for low in range(targets[0], targets[1], TGT_BLOCK):
            to = slice(low, low + TGT_BLOCK)
            radius_sq = lax.dot_general(
                rows, target_ref[:, to], (((0,), (0,)), ((), ())), preferred_element_type=F32
            )
            inverse = lax.rsqrt(radius_sq)
            square = inverse * inverse
            fifth = square * square * inverse
            head = fifth.astype(BF16)
            tail = (fifth - head.astype(F32)).astype(BF16)
            if kept is not None:
                kept[0][at, to] = head
                kept[1][at, to] = tail
            add_sums(weights, head, tail, acc_ref, to)


def add_kept(kept, weights_ref, acc_ref, first, count, targets):
    at = span(first, count)
    weights = weights_ref[:, at]
    for low in range(targets[0], targets[1], TGT_BLOCK):
        to = slice(low, low + TGT_BLOCK)
        add_sums(weights, kept[0][at, to], kept[1][at, to], acc_ref, to)


def picked(table, high, low, first=0):
    out = None
    for group, row in enumerate(table):
        found = jnp.take_along_axis(row, low, axis=1)
        out = found if out is None else jnp.where(high == first + group, found, out)
    return out


def dot3(a, b):
    return a[0] * b[0] + a[1] * b[1] + a[2] * b[2]


def geometry(mine, other, live):
    sep = [mine[k] - other[k] for k in range(3)]
    vel = [mine[3 + k] - other[3 + k] for k in range(3)]
    radius_sq = dot3(sep, sep) + 1.0
    inverse = lax.rsqrt(radius_sq)
    normal = [jnp.where(live, s * inverse, 0.0) for s in sep]
    return normal + [-0.03 * (radius_sq * inverse - 1.0) - 0.5 * dot3(vel, normal)]


def pair_force(normal, along, m_one, m_two):
    one = dot3(m_one, normal)
    two = dot3(m_two, normal)
    radial = 3.0 * (dot3(m_one, m_two) - 5.0 * one * two) + along
    return [3.0 * (one * m_two[k] + two * m_one[k]) + radial * normal[k] for k in range(3)]


def scatter_to(acc_ref, force, high, low):
    group_ids = lax.broadcasted_iota(jnp.int32, (8, 128), 0)
    lane_ids = lax.broadcasted_iota(jnp.int32, (128, 128), 0)
    split = [p for f in force for p in pieces(f, 3)]
    left, right = [], []
    for k in range(8):
        hit = jnp.broadcast_to(high[k : k + 1], (8, 128)) == group_ids
        left.append(
            jnp.concatenate(
                [jnp.where(hit, jnp.broadcast_to(p[k : k + 1], (8, 128)), 0.0) for p in split], axis=0
            ).astype(BF16)
        )
        same = jnp.broadcast_to(low[k : k + 1], (128, 128)) == lane_ids
        right.append(jnp.where(same, 1.0, 0.0).astype(BF16))
    acc_ref[...] += lax.dot_general(
        jnp.concatenate(left, axis=1),
        jnp.concatenate(right, axis=1),
        (((1,), (1,)), ((), ())),
        preferred_element_type=F32,
    )


def two_by_two(low, high, body):
    @pl.loop(low // 2, high // 2)
    def _(index):
        body(2 * index)
        body(2 * index + 1)


def induce(
    pos_ref, vel_ref, app_ref, sus_ref, raw_ref, part_ref, count_ref,
    mom_ref, force_ref,
    pos_cols, vel_cols, mom_cols, own_ref, own_back, part_back, geo_ref, near_ref, far_ref, sums_ref,
    block_ref, block_all, first_ref, first_all, second_ref, rows_ref, weights_ref, target_ref, acc_ref, heads, tails,
    row_send, row_recv, one_send, one_recv, col_send, col_recv, two_send, two_recv, local_sem,
):
    length = pos_ref.shape[1]
    half = length // 2
    parts = block_all.shape[0]
    here = lax.axis_index("row")
    column = lax.axis_index("col")

    enter()
    pos = pos_ref[...] - CENTRE
    start = sus_ref[...] * app_ref[...]
    block_ref[0:3, :] = pos
    block_ref[3:6, :] = start
    target_ref[...] = target_rows(pos)
    acc_ref[...] = jnp.zeros_like(acc_ref)
    kept = (heads, tails)
    sums_ref[...] = jnp.zeros_like(sums_ref)
    columns, slots = raw_ref.shape
    on_diagonal = lax.broadcasted_iota(jnp.int32, (columns, columns), 0) == lax.broadcasted_iota(
        jnp.int32, (columns, columns), 1
    )
    counts = jnp.sum(
        jnp.where(on_diagonal, jnp.broadcast_to(count_ref[...], (columns, columns)).astype(F32), 0.0),
        axis=1, keepdims=True,
    )
    slot_ids = lax.broadcasted_iota(jnp.int32, (columns, slots), 1).astype(F32)
    own_ref[...] = jnp.where(slot_ids < counts, raw_ref[...], -1)

    def row_copy(source, gathered, send, recv, step):
        to = row_steps(step)[0]
        return pltpu.make_async_remote_copy(
            src_ref=source, dst_ref=gathered.at[here], send_sem=send.at[step], recv_sem=recv.at[step],
            device_id={"row": to}, device_id_type=MESH,
        )

    def row_arrival(source, gathered, send, recv, step):
        to, origin = row_steps(step)
        return pltpu.make_async_remote_copy(
            src_ref=source, dst_ref=gathered.at[origin], send_sem=send.at[step], recv_sem=recv.at[step],
            device_id={"row": to}, device_id_type=MESH,
        )

    row_args = (block_ref, block_all, row_send, row_recv)
    one_args = (first_ref, first_all, one_send, one_recv)
    def col_pairs(to, origin):
        return (
            (pos_ref, pos_cols.at[:, origin, :]),
            (vel_ref, vel_cols.at[:, origin, :]),
            (own_ref.at[pl.ds(to, 1)], own_back.at[pl.ds(origin, 1)]),
            (part_ref.at[pl.ds(to, 1)], part_back.at[pl.ds(origin, 1)]),
        )

    def col_copies(to, origin, step):
        return [
            pltpu.make_async_remote_copy(
                src_ref=source, dst_ref=target, send_sem=col_send.at[k, step], recv_sem=col_recv.at[k, step],
                device_id={"col": to}, device_id_type=MESH,
            )
            for k, (source, target) in enumerate(col_pairs(to, origin))
        ]

    def col_start(step):
        for copy in col_copies(col_steps(step)[0], column, step):
            copy.start()

    def own_copies():
        return [
            pltpu.make_async_copy(source, target, local_sem.at[k])
            for k, (source, target) in enumerate(col_pairs(column, column))
        ]

    def two_copy(part, to, origin, step):
        return pltpu.make_async_remote_copy(
            src_ref=second_ref.at[part], dst_ref=mom_cols.at[part, :, origin, :],
            send_sem=two_send.at[part, step], recv_sem=two_recv.at[part, step],
            device_id={"col": to}, device_id_type=MESH,
        )

    def two_own(part):
        return pltpu.make_async_copy(second_ref.at[part], mom_cols.at[part, :, column, :], local_sem.at[4 + part])

    def two_start(part):
        every_step("col", lambda step: two_copy(part, col_steps(step)[0], column, step).start())
        two_own(part).start()

    def prepare(step, pos, mom, with_rows):
        at = span(step * length, length)
        if with_rows:
            rows_ref[:, at] = source_rows(pos)
        weights_ref[:, at] = source_weights(pos, mom)

    prepare(0, pos, start, True)
    add_field(rows_ref, weights_ref, target_ref, acc_ref, 0, length, (0, half), kept)
    pl.semaphore_wait(pltpu.get_barrier_semaphore(), lax.axis_size("row") + lax.axis_size("col") - 2)
    every_step("row", lambda step: row_copy(*row_args, step).start())

    def wait_first(step):
        row_arrival(*row_args, step).wait_recv()

    def take_first(step):
        origin = row_steps(step)[1]
        prepare(step, block_all[origin, 0:3, :], block_all[origin, 3:6, :], True)

    add_field(rows_ref, weights_ref, target_ref, acc_ref, 0, length, (half, length), kept)
    wait_first(1)
    take_first(1)

    @pl.loop(1, KEPT)
    def _(step):
        @pl.when(step == 4)
        def _():
            each_step("col", col_start)
            for copy in own_copies():
                copy.start()

        wait_first(step + 1)
        add_field(rows_ref, weights_ref, target_ref, acc_ref, step * length, length, (0, length), kept)
        take_first(step + 1)

    for step in range(KEPT, parts):
        if step + 1 < parts:
            wait_first(step + 1)
        add_field(rows_ref, weights_ref, target_ref, acc_ref, step * length, length, (0, length))
        if step + 1 < parts:
            take_first(step + 1)

    field = combine(acc_ref[...], pos)
    first = sus_ref[...] * (app_ref[...] + (field + start))
    first_ref[...] = first
    prepare(0, pos, first, False)
    acc_ref[...] = jnp.zeros_like(acc_ref)
    every_step("row", lambda step: row_copy(*one_args, step).start())

    chunks = slots // 128
    units = columns // 8 * chunks
    groups = [slice(g * 128, g * 128 + 128) for g in range(length // 128)]
    split_at = len(groups) // 2

    def lists(unit):
        eight = pl.ds(pl.multiple_of(lax.div(unit, chunks) * 8, 8), 8)
        at = pl.ds(pl.multiple_of(lax.rem(unit, chunks) * 128, 128), 128)
        here_own, here_part = own_ref[eight, at], part_ref[eight, at]
        back_own, back_part = own_back[eight, at], part_back[eight, at]
        return eight, ((here_own, here_part, here_own >= 0), (back_part, back_own, back_own >= 0))

    def spread(ref, j):
        return [jnp.broadcast_to(ref[j : j + 1, g], (8, 128)) for g in groups]

    def halves(part, j, eight):
        return [mom_cols[part, j, eight, groups[g]] for g in range(split_at)]

    def col_done(step):
        to, origin = col_steps(step)
        for copy in col_copies(to, origin, step):
            copy.wait()

    each_step("col", col_done)
    for copy in own_copies():
        copy.wait()

    def pair_geometry(unit):
        eight, both = lists(unit)
        for which, (my_ids, other_ids, live) in enumerate(both):
            mine, other = [], []
            for near, far in ((pos_ref, pos_cols), (vel_ref, vel_cols)):
                for j in range(3):
                    mine.append(picked(spread(near, j), my_ids >> 7, my_ids & 127))
                    other.append(picked([far[j, eight, g] for g in groups], other_ids >> 7, other_ids & 127))
            for k, value in enumerate(geometry(mine, other, live)):
                geo_ref[unit, which, k] = value

    two_by_two(0, EARLY, pair_geometry)

    def finish(part):
        at = slice(part * half, part * half + half)
        field = combine(acc_ref[:, at], pos_ref[:, at] - CENTRE)
        second = sus_ref[:, at] * (app_ref[:, at] + (field + first_ref[:, at]))
        second_ref[part] = second
        mom_ref[:, at] = second

    def wait_second(step):
        row_arrival(*one_args, step).wait_recv()

    def take_second(step):
        origin = row_steps(step)[1]
        prepare(step, block_all[origin, 0:3, :], first_all[origin], False)

    @pl.loop(0, KEPT)
    def _(step):
        wait_second(step + 1)
        add_kept(kept, weights_ref, acc_ref, step * length, length, (0, half))
        take_second(step + 1)

    for step in range(KEPT, parts):
        if step + 1 < parts:
            wait_second(step + 1)
        add_field(rows_ref, weights_ref, target_ref, acc_ref, step * length, length, (0, half))
        if step + 1 < parts:
            take_second(step + 1)

    finish(0)

    @pl.loop(0, KEPT // 2)
    def _(step):
        @pl.when(step == 1)
        def _():
            two_start(0)

        add_kept(kept, weights_ref, acc_ref, step * 2 * length, 2 * length, (half, length))

    add_field(rows_ref, weights_ref, target_ref, acc_ref, KEPT * length, (parts - KEPT) * length, (half, length))
    finish(1)

    def row_done(step):
        row_copy(*row_args, step).wait_send()
        row_copy(*one_args, step).wait_send()

    each_step("row", row_done)
    two_start(1)


    def two_done(part):
        each_step("col", lambda step: two_copy(part, *col_steps(step), step).wait())
        two_own(part).wait()

    two_by_two(EARLY, units, pair_geometry)
    two_done(0)

    def own_moments(unit):
        eight, both = lists(unit)
        for which, (my_ids, other_ids, live) in enumerate(both):
            for j in range(3):
                near_ref[unit, which, j] = picked(spread(mom_ref, j), my_ids >> 7, my_ids & 127)
                far_ref[unit, which, j] = picked(halves(0, j, eight), other_ids >> 7, other_ids & 127)

    two_by_two(0, units, own_moments)
    two_done(1)

    def slot_forces(unit):
        eight, both = lists(unit)
        for which, (my_ids, other_ids, live) in enumerate(both):
            high, low = other_ids >> 7, other_ids & 127
            theirs = [
                jnp.where(high < split_at, far_ref[unit, which, j], picked(halves(1, j, eight), high, low, split_at))
                for j in range(3)
            ]
            ours = [near_ref[unit, which, j] for j in range(3)]
            normal = [geo_ref[unit, which, k] for k in range(3)]
            force = pair_force(normal, geo_ref[unit, which, 3], ours, theirs)
            scatter_to(sums_ref.at[which], force, my_ids >> 7, my_ids & 127)

    two_by_two(0, units, slot_forces)
    totals = sums_ref[0] + sums_ref[1]

    for k in range(3):
        base = 24 * k
        total = totals[base : base + 8] + (totals[base + 8 : base + 16] + totals[base + 16 : base + 24])
        for g in range(8):
            force_ref[k : k + 1, groups[g]] = total[g : g + 1]


def on_device(positions, velocity, applied, suscept, contact_owner, contact_partner, contact_count):
    rows = lax.axis_size("row")
    cols = lax.axis_size("col")
    length = positions.shape[1]
    slots = contact_owner.shape[3]
    copies = pltpu.SemaphoreType.DMA
    vector = jax.ShapeDtypeStruct((3, length), F32)
    units = cols // 8 * (slots // 128)
    return pl.pallas_call(
        induce,
        out_shape=(vector, vector),
        in_specs=vmem_specs(7),
        out_specs=tuple(vmem_specs(2)),
        scratch_shapes=[
            pltpu.VMEM((3, cols, length), F32),
            pltpu.VMEM((3, cols, length), F32),
            pltpu.VMEM((2, 3, cols, length // 2), F32),
            pltpu.VMEM((cols, slots), jnp.int32),
            pltpu.VMEM((cols, slots), jnp.int32),
            pltpu.VMEM((cols, slots), jnp.int32),
            pltpu.VMEM((units, 2, 4, 8, 128), F32),
            pltpu.VMEM((units, 2, 3, 8, 128), F32),
            pltpu.VMEM((units, 2, 3, 8, 128), F32),
            pltpu.VMEM((2, 72, 128), F32),
            pltpu.VMEM((6, length), F32),
            pltpu.VMEM((rows, 6, length), F32),
            pltpu.VMEM((3, length), F32),
            pltpu.VMEM((rows, 3, length), F32),
            pltpu.VMEM((2, 3, length // 2), F32),
            pltpu.VMEM((24, rows * length), BF16),
            pltpu.VMEM((45, rows * length), BF16),
            pltpu.VMEM((24, length), BF16),
            pltpu.VMEM((45, length), F32),
            pltpu.VMEM((KEPT * length, length), BF16),
            pltpu.VMEM((KEPT * length, length), BF16),
            copies((rows,)), copies((rows,)), copies((rows,)), copies((rows,)),
            copies((4, cols)), copies((4, cols)), copies((2, cols)), copies((2, cols)),
            copies((6,)),
        ],
        compiler_params=pltpu.CompilerParams(
            collective_id=0, has_side_effects=True, vmem_limit_bytes=67043328
        ),
        name="induce",
    )(
        positions, velocity, applied, suscept.reshape(1, length),
        contact_owner.reshape(cols, slots), contact_partner.reshape(cols, slots), contact_count.reshape(1, cols),
    )


def solution(mesh):
    placed = (
        P(None, ("col", "row")),
        P(None, ("col", "row")),
        P(None, ("col", "row")),
        P(("col", "row")),
        P("col", "row", None, None),
        P("col", "row", None, None),
        P("col", "row", None),
    )
    return jax.shard_map(
        on_device,
        mesh=mesh,
        in_specs=placed,
        out_specs=(P(None, ("col", "row")), P(None, ("col", "row"))),
        check_vma=False,
    )
```

```python
import functools

import jax
import jax.numpy as jnp
from jax import lax
from jax.experimental import pallas as pl
from jax.experimental.pallas import tpu as pltpu
from jax.sharding import PartitionSpec as P

F32 = jnp.float32
BF16 = jnp.bfloat16
MESH = pl.DeviceIdType.MESH
CENTRE = 8.0
SRC_BLOCK = 512
ROW_SHAPE = (2, 4, 2)
COL_SHAPE = (4, 4)
KEPT = 14
TAIL_ROWS = 32
EARLY = 4
TGT_BLOCK = 256


def vmem_specs(count):
    return [pl.BlockSpec(memory_space=pltpu.VMEM)] * count


def row_steps(step):
    depth, height, cores = ROW_SHAPE
    me = lax.axis_index("row")
    core, rest = lax.rem(me, cores), lax.div(me, cores)
    y, z = lax.rem(rest, height), lax.div(rest, height)
    core_by, rest_by = lax.rem(step, cores), lax.div(step, cores)
    turn, z_by = lax.rem(rest_by, height), lax.div(rest_by, height)
    y_by = turn + lax.div(turn, 2) - 2 * lax.div(turn, 3)

    def at(sign):
        new_z = lax.rem(z + depth + sign * z_by, depth)
        new_y = lax.rem(y + height + sign * y_by, height)
        new_core = lax.rem(core + cores + sign * core_by, cores)
        return (new_z * height + new_y) * cores + new_core

    return at(1), at(-1)


def col_steps(step):
    wide, deep = COL_SHAPE
    me = lax.axis_index("col")
    x, z = lax.div(me, deep), lax.rem(me, deep)
    if isinstance(step, int):
        x_by, z_by = step // deep, step % deep
    else:
        x_by, z_by = lax.div(step, deep), lax.rem(step, deep)

    def at(sign):
        return lax.rem(x + wide + sign * x_by, wide) * deep + lax.rem(z + deep + sign * z_by, deep)

    return at(1), at(-1)


def far_first():
    wide, deep = COL_SHAPE

    def hops(step):
        x_by, z_by = step // deep, step % deep
        return 2 * min(z_by, deep - z_by) + min(x_by, wide - x_by)

    return sorted(range(1, wide * deep), key=hops, reverse=True)


def each_step(axis, body):
    lax.fori_loop(1, lax.axis_size(axis), lambda step, carry: (body(step), carry)[1], 0)


def every_step(axis, body):
    for step in range(1, lax.axis_size(axis)):
        body(step)


def enter():
    barrier = pltpu.get_barrier_semaphore()

    def signal_row(step):
        pl.semaphore_signal(barrier, inc=1, device_id={"row": row_steps(step)[0]}, device_id_type=MESH)

    def signal_col(step):
        pl.semaphore_signal(barrier, inc=1, device_id={"col": col_steps(step)[0]}, device_id_type=MESH)

    every_step("row", signal_row)
    every_step("col", signal_col)


def pieces(value, count):
    out = []
    for unused in range(count):
        head = value.astype(BF16)
        wide = head.astype(F32)
        out.append(wide)
        value = value - wide
    return out


def target_rows(pos):
    first, second, third = pieces(-2.0 * pos, 3)
    norm = jnp.sum(pos * pos, axis=0, keepdims=True) + 1.0
    one = jnp.ones_like(norm)
    rows = [first, second, third, first, second, first, one, one, one] + pieces(norm, 3)
    return jnp.concatenate(rows, axis=0).astype(BF16)


def source_rows(pos):
    first, second, third = pieces(pos, 3)
    norm = jnp.sum(pos * pos, axis=0, keepdims=True)
    one = jnp.ones_like(norm)
    rows = [first, first, first, second, second, third] + pieces(norm, 3) + [one, one, one]
    return jnp.concatenate(rows, axis=0).astype(BF16)


def source_weights(pos, mom):
    norm = jnp.sum(pos * pos, axis=0, keepdims=True)
    along = jnp.sum(pos * mom, axis=0, keepdims=True)
    terms = jnp.concatenate(
        [mom, pos[0:1] * mom, pos[1:2] * mom, pos[2:3] * mom, 3.0 * (along * pos) - norm * mom], axis=0
    )
    return jnp.concatenate(pieces(terms, 3), axis=0).astype(BF16)


def combine(acc, pos):
    sums = acc[0:15] + (acc[15:30] + acc[30:45])
    x, y, z = pos[0:1], pos[1:2], pos[2:3]
    mom = sums[0:3]
    by_x, by_y, by_z = sums[3:6], sums[6:9], sums[9:12]
    mixed = sums[12:15]
    inner = x * mom[0:1] + y * mom[1:2] + z * mom[2:3]
    trace = by_x[0:1] + by_y[1:2] + by_z[2:3]
    crossed = jnp.concatenate(
        [x * by[0:1] + y * by[1:2] + z * by[2:3] for by in (by_x, by_y, by_z)], axis=0
    )
    radial = pos * (inner - trace) - crossed
    norm = jnp.sum(pos * pos, axis=0, keepdims=True) + 1.0
    direct = norm * mom - 2.0 * (x * by_x + y * by_y + z * by_z)
    return 3.0 * radial - direct + mixed


def span(start, size):
    return pl.ds(start if isinstance(start, int) else pl.multiple_of(start, size), size)


def add_sums(weights, head, tail, acc_ref, to):
    acc_ref[:, to] += jnp.dot(weights, head, preferred_element_type=F32)
    acc_ref[0:TAIL_ROWS, to] += jnp.dot(weights[0:TAIL_ROWS], tail, preferred_element_type=F32)


def add_field(rows_ref, weights_ref, target_ref, acc_ref, first, count, targets, kept=None):
    for start in range(0, count, SRC_BLOCK):
        at = span(first + start, SRC_BLOCK)
        rows = rows_ref[:, at]
        weights = weights_ref[:, at]
        for low in range(targets[0], targets[1], TGT_BLOCK):
            to = slice(low, low + TGT_BLOCK)
            radius_sq = lax.dot_general(
                rows, target_ref[:, to], (((0,), (0,)), ((), ())), preferred_element_type=F32
            )
            inverse = lax.rsqrt(radius_sq)
            square = inverse * inverse
            fifth = square * square * inverse
            head = fifth.astype(BF16)
            tail = (fifth - head.astype(F32)).astype(BF16)
            if kept is not None:
                kept[0][at, to] = head
                kept[1][at, to] = tail
            add_sums(weights, head, tail, acc_ref, to)


def add_kept(kept, weights_ref, acc_ref, first, count, targets):
    at = span(first, count)
    weights = weights_ref[:, at]
    for low in range(targets[0], targets[1], TGT_BLOCK):
        to = slice(low, low + TGT_BLOCK)
        add_sums(weights, kept[0][at, to], kept[1][at, to], acc_ref, to)


def picked(table, high, low, first=0):
    out = None
    for group, row in enumerate(table):
        found = jnp.take_along_axis(row, low, axis=1)
        out = found if out is None else jnp.where(high == first + group, found, out)
    return out


def dot3(a, b):
    return a[0] * b[0] + a[1] * b[1] + a[2] * b[2]


def geometry(mine, other, live):
    sep = [mine[k] - other[k] for k in range(3)]
    vel = [mine[3 + k] - other[3 + k] for k in range(3)]
    radius_sq = dot3(sep, sep) + 1.0
    inverse = lax.rsqrt(radius_sq)
    normal = [jnp.where(live, s * inverse, 0.0) for s in sep]
    return normal + [-0.03 * (radius_sq * inverse - 1.0) - 0.5 * dot3(vel, normal)]


def pair_force(normal, along, m_one, m_two):
    one = dot3(m_one, normal)
    two = dot3(m_two, normal)
    radial = 3.0 * (dot3(m_one, m_two) - 5.0 * one * two) + along
    return [3.0 * (one * m_two[k] + two * m_one[k]) + radial * normal[k] for k in range(3)]


def scatter_to(acc_ref, force, high, low):
    group_ids = lax.broadcasted_iota(jnp.int32, (8, 128), 0)
    lane_ids = lax.broadcasted_iota(jnp.int32, (128, 128), 0)
    split = [p for f in force for p in pieces(f, 3)]
    left, right = [], []
    for k in range(8):
        hit = jnp.broadcast_to(high[k : k + 1], (8, 128)) == group_ids
        left.append(
            jnp.concatenate(
                [jnp.where(hit, jnp.broadcast_to(p[k : k + 1], (8, 128)), 0.0) for p in split], axis=0
            ).astype(BF16)
        )
        same = jnp.broadcast_to(low[k : k + 1], (128, 128)) == lane_ids
        right.append(jnp.where(same, 1.0, 0.0).astype(BF16))
    acc_ref[...] += lax.dot_general(
        jnp.concatenate(left, axis=1),
        jnp.concatenate(right, axis=1),
        (((1,), (1,)), ((), ())),
        preferred_element_type=F32,
    )


def two_by_two(low, high, body):
    @pl.loop(low // 2, high // 2)
    def _(index):
        body(2 * index)
        body(2 * index + 1)


def induce(
    pos_ref, vel_ref, app_ref, sus_ref, raw_ref, part_ref, count_ref,
    both_ref,
    pos_cols, vel_cols, mom_cols, own_ref, own_back, part_back, geo_ref, near_ref, far_ref, sums_ref,
    block_ref, block_all, first_ref, first_all, second_ref, rows_ref, weights_ref, target_ref, acc_ref, heads, tails,
    row_send, row_recv, one_send, one_recv, col_send, col_recv, two_send, two_recv, local_sem,
):
    length = pos_ref.shape[1]
    half = length // 2
    parts = block_all.shape[0]
    here = lax.axis_index("row")
    column = lax.axis_index("col")

    mom_ref, force_ref = both_ref.at[0], both_ref.at[1]
    enter()
    pos = pos_ref[...] - CENTRE
    start = sus_ref[...] * app_ref[...]
    block_ref[0:3, :] = pos
    block_ref[3:6, :] = start
    target_ref[...] = target_rows(pos)
    acc_ref[...] = jnp.zeros_like(acc_ref)
    kept = (heads, tails)
    sums_ref[...] = jnp.zeros_like(sums_ref)
    columns, slots = raw_ref.shape
    on_diagonal = lax.broadcasted_iota(jnp.int32, (columns, columns), 0) == lax.broadcasted_iota(
        jnp.int32, (columns, columns), 1
    )
    counts = jnp.sum(
        jnp.where(on_diagonal, jnp.broadcast_to(count_ref[...], (columns, columns)).astype(F32), 0.0),
        axis=1, keepdims=True,
    )
    slot_ids = lax.broadcasted_iota(jnp.int32, (columns, slots), 1).astype(F32)
    own_ref[...] = jnp.where(slot_ids < counts, raw_ref[...], -1)

    def row_copy(source, gathered, send, recv, step):
        to = row_steps(step)[0]
        return pltpu.make_async_remote_copy(
            src_ref=source, dst_ref=gathered.at[here], send_sem=send.at[step], recv_sem=recv.at[step],
            device_id={"row": to}, device_id_type=MESH,
        )

    def row_arrival(source, gathered, send, recv, step):
        to, origin = row_steps(step)
        return pltpu.make_async_remote_copy(
            src_ref=source, dst_ref=gathered.at[origin], send_sem=send.at[step], recv_sem=recv.at[step],
            device_id={"row": to}, device_id_type=MESH,
        )

    row_args = (block_ref, block_all, row_send, row_recv)
    one_args = (first_ref, first_all, one_send, one_recv)
    def col_pairs(to, origin):
        return (
            (pos_ref, pos_cols.at[:, origin, :]),
            (vel_ref, vel_cols.at[:, origin, :]),
            (own_ref.at[pl.ds(to, 1)], own_back.at[pl.ds(origin, 1)]),
            (part_ref.at[pl.ds(to, 1)], part_back.at[pl.ds(origin, 1)]),
        )

    def col_copies(to, origin, step):
        return [
            pltpu.make_async_remote_copy(
                src_ref=source, dst_ref=target, send_sem=col_send.at[k, step], recv_sem=col_recv.at[k, step],
                device_id={"col": to}, device_id_type=MESH,
            )
            for k, (source, target) in enumerate(col_pairs(to, origin))
        ]

    def col_start(step):
        for copy in col_copies(col_steps(step)[0], column, step):
            copy.start()

    def own_copies():
        return [
            pltpu.make_async_copy(source, target, local_sem.at[k])
            for k, (source, target) in enumerate(col_pairs(column, column))
        ]

    def two_copy(part, to, origin, step):
        return pltpu.make_async_remote_copy(
            src_ref=second_ref.at[part], dst_ref=mom_cols.at[part, :, origin, :],
            send_sem=two_send.at[part, step], recv_sem=two_recv.at[part, step],
            device_id={"col": to}, device_id_type=MESH,
        )

    def two_own(part):
        return pltpu.make_async_copy(second_ref.at[part], mom_cols.at[part, :, column, :], local_sem.at[4 + part])

    def two_start(part):
        for step in far_first():
            two_copy(part, col_steps(step)[0], column, step).start()
        two_own(part).start()

    def prepare(step, pos, mom, with_rows):
        at = span(step * length, length)
        if with_rows:
            rows_ref[:, at] = source_rows(pos)
        weights_ref[:, at] = source_weights(pos, mom)

    prepare(0, pos, start, True)
    add_field(rows_ref, weights_ref, target_ref, acc_ref, 0, length, (0, half), kept)
    pl.semaphore_wait(pltpu.get_barrier_semaphore(), lax.axis_size("row") + lax.axis_size("col") - 2)
    every_step("row", lambda step: row_copy(*row_args, step).start())

    def wait_first(step):
        row_arrival(*row_args, step).wait_recv()

    def take_first(step):
        origin = row_steps(step)[1]
        prepare(step, block_all[origin, 0:3, :], block_all[origin, 3:6, :], True)

    add_field(rows_ref, weights_ref, target_ref, acc_ref, 0, length, (half, length), kept)
    wait_first(1)
    take_first(1)

    @pl.loop(1, KEPT)
    def _(step):
        @pl.when(step == 4)
        def _():
            each_step("col", col_start)
            for copy in own_copies():
                copy.start()

        wait_first(step + 1)
        add_field(rows_ref, weights_ref, target_ref, acc_ref, step * length, length, (0, length), kept)
        take_first(step + 1)

    for step in range(KEPT, parts):
        if step + 1 < parts:
            wait_first(step + 1)
        add_field(rows_ref, weights_ref, target_ref, acc_ref, step * length, length, (0, length))
        if step + 1 < parts:
            take_first(step + 1)

    field = combine(acc_ref[...], pos)
    first = sus_ref[...] * (app_ref[...] + (field + start))
    first_ref[...] = first
    prepare(0, pos, first, False)
    acc_ref[...] = jnp.zeros_like(acc_ref)
    every_step("row", lambda step: row_copy(*one_args, step).start())

    chunks = slots // 128
    units = columns // 8 * chunks
    groups = [slice(g * 128, g * 128 + 128) for g in range(length // 128)]
    split_at = len(groups) // 2

    def lists(unit):
        eight = pl.ds(pl.multiple_of(lax.div(unit, chunks) * 8, 8), 8)
        at = pl.ds(pl.multiple_of(lax.rem(unit, chunks) * 128, 128), 128)
        here_own, here_part = own_ref[eight, at], part_ref[eight, at]
        back_own, back_part = own_back[eight, at], part_back[eight, at]
        return eight, ((here_own, here_part, here_own >= 0), (back_part, back_own, back_own >= 0))

    def spread(ref, j):
        return [jnp.broadcast_to(ref[j : j + 1, g], (8, 128)) for g in groups]

    def halves(part, j, eight):
        return [mom_cols[part, j, eight, groups[g]] for g in range(split_at)]

    def col_done(step):
        to, origin = col_steps(step)
        for copy in col_copies(to, origin, step):
            copy.wait()

    each_step("col", col_done)
    for copy in own_copies():
        copy.wait()

    def pair_geometry(unit):
        eight, both = lists(unit)
        for which, (my_ids, other_ids, live) in enumerate(both):
            mine, other = [], []
            for near, far in ((pos_ref, pos_cols), (vel_ref, vel_cols)):
                for j in range(3):
                    mine.append(picked(spread(near, j), my_ids >> 7, my_ids & 127))
                    other.append(picked([far[j, eight, g] for g in groups], other_ids >> 7, other_ids & 127))
            for k, value in enumerate(geometry(mine, other, live)):
                geo_ref[unit, which, k] = value

    two_by_two(0, EARLY, pair_geometry)

    def finish(part):
        at = slice(part * half, part * half + half)
        field = combine(acc_ref[:, at], pos_ref[:, at] - CENTRE)
        second = sus_ref[:, at] * (app_ref[:, at] + (field + first_ref[:, at]))
        second_ref[part] = second
        mom_ref[:, at] = second

    def wait_second(step):
        row_arrival(*one_args, step).wait_recv()

    def take_second(step):
        origin = row_steps(step)[1]
        prepare(step, block_all[origin, 0:3, :], first_all[origin], False)

    @pl.loop(0, KEPT)
    def _(step):
        wait_second(step + 1)
        add_kept(kept, weights_ref, acc_ref, step * length, length, (0, half))
        take_second(step + 1)

    for step in range(KEPT, parts):
        if step + 1 < parts:
            wait_second(step + 1)
        add_field(rows_ref, weights_ref, target_ref, acc_ref, step * length, length, (0, half))
        if step + 1 < parts:
            take_second(step + 1)

    finish(0)

    @pl.loop(0, KEPT // 2)
    def _(step):
        @pl.when(step == 1)
        def _():
            two_start(0)

        add_kept(kept, weights_ref, acc_ref, step * 2 * length, 2 * length, (half, length))

    add_field(rows_ref, weights_ref, target_ref, acc_ref, KEPT * length, (parts - KEPT) * length, (half, length))
    finish(1)

    each_step("row", lambda step: row_copy(*row_args, step).wait_send())
    two_start(1)
    each_step("row", lambda step: row_copy(*one_args, step).wait_send())


    def two_done(part):
        each_step("col", lambda step: two_copy(part, *col_steps(step), step).wait())
        two_own(part).wait()

    two_by_two(EARLY, units, pair_geometry)
    two_done(0)

    def own_moments(unit):
        eight, both = lists(unit)
        for which, (my_ids, other_ids, live) in enumerate(both):
            for j in range(3):
                near_ref[unit, which, j] = picked(spread(mom_ref, j), my_ids >> 7, my_ids & 127)
                far_ref[unit, which, j] = picked(halves(0, j, eight), other_ids >> 7, other_ids & 127)

    two_by_two(0, units, own_moments)
    two_done(1)

    def slot_forces(unit):
        eight, both = lists(unit)
        for which, (my_ids, other_ids, live) in enumerate(both):
            high, low = other_ids >> 7, other_ids & 127
            theirs = [
                jnp.where(high < split_at, far_ref[unit, which, j], picked(halves(1, j, eight), high, low, split_at))
                for j in range(3)
            ]
            ours = [near_ref[unit, which, j] for j in range(3)]
            normal = [geo_ref[unit, which, k] for k in range(3)]
            force = pair_force(normal, geo_ref[unit, which, 3], ours, theirs)
            scatter_to(sums_ref.at[which], force, my_ids >> 7, my_ids & 127)

    two_by_two(0, units, slot_forces)
    totals = sums_ref[0] + sums_ref[1]

    for k in range(3):
        base = 24 * k
        total = totals[base : base + 8] + (totals[base + 8 : base + 16] + totals[base + 16 : base + 24])
        for g in range(8):
            force_ref[k : k + 1, groups[g]] = total[g : g + 1]


def on_device(positions, velocity, applied, suscept, contact_owner, contact_partner, contact_count):
    rows = lax.axis_size("row")
    cols = lax.axis_size("col")
    length = positions.shape[1]
    slots = contact_owner.shape[3]
    copies = pltpu.SemaphoreType.DMA
    units = cols // 8 * (slots // 128)
    both = pl.pallas_call(
        induce,
        out_shape=jax.ShapeDtypeStruct((2, 3, length), F32),
        in_specs=vmem_specs(7),
        out_specs=pl.BlockSpec(memory_space=pltpu.VMEM),
        scratch_shapes=[
            pltpu.VMEM((3, cols, length), F32),
            pltpu.VMEM((3, cols, length), F32),
            pltpu.VMEM((2, 3, cols, length // 2), F32),
            pltpu.VMEM((cols, slots), jnp.int32),
            pltpu.VMEM((cols, slots), jnp.int32),
            pltpu.VMEM((cols, slots), jnp.int32),
            pltpu.VMEM((units, 2, 4, 8, 128), F32),
            pltpu.VMEM((units, 2, 3, 8, 128), F32),
            pltpu.VMEM((units, 2, 3, 8, 128), F32),
            pltpu.VMEM((2, 72, 128), F32),
            pltpu.VMEM((6, length), F32),
            pltpu.VMEM((rows, 6, length), F32),
            pltpu.VMEM((3, length), F32),
            pltpu.VMEM((rows, 3, length), F32),
            pltpu.VMEM((2, 3, length // 2), F32),
            pltpu.VMEM((24, rows * length), BF16),
            pltpu.VMEM((45, rows * length), BF16),
            pltpu.VMEM((24, length), BF16),
            pltpu.VMEM((45, length), F32),
            pltpu.VMEM((KEPT * length, length), BF16),
            pltpu.VMEM((KEPT * length, length), BF16),
            copies((rows,)), copies((rows,)), copies((rows,)), copies((rows,)),
            copies((4, cols)), copies((4, cols)), copies((2, cols)), copies((2, cols)),
            copies((6,)),
        ],
        compiler_params=pltpu.CompilerParams(
            collective_id=0, has_side_effects=True, vmem_limit_bytes=67043328
        ),
        name="induce",
    )(
        positions, velocity, applied, suscept.reshape(1, length),
        contact_owner.reshape(cols, slots), contact_partner.reshape(cols, slots), contact_count.reshape(1, cols),
    )
    return (both[0], both[1])


def solution(mesh):
    placed = (
        P(None, ("col", "row")),
        P(None, ("col", "row")),
        P(None, ("col", "row")),
        P(("col", "row")),
        P("col", "row", None, None),
        P("col", "row", None, None),
        P("col", "row", None),
    )
    return jax.shard_map(
        on_device,
        mesh=mesh,
        in_specs=placed,
        out_specs=(P(None, ("col", "row")), P(None, ("col", "row"))),
        check_vma=False,
    )
```
